32 devices in a mesh: groups: 2 (over x), dom: 16 (over z, y, core).
Axes of the slice: x: 2, y: 2, z: 4, core: 2. Of those that a mesh axis runs over, the one named last changes fastest.
Arguments:
- particle_places: float32 [16, 3, 3072], P('groups', None, 'dom'), parts along dimension 0, may hold values from 0 to 48, as said below
- particle_speeds: float32 [16, 3, 3072], P('groups', None, 'dom'), parts along dimension 0, may hold values from -7 to 7
- thermal_targets: float32 [16], P('groups'), parts along dimension 0, may hold values from 0.5 to 2
- element_features: bfloat16 [6144, 128], P(('groups', 'dom')), parts along dimension 0, may hold values from -4 to 4
- swap_counterpart_slot: int32 [16], P('groups'), parts along dimension 0, may hold values from 0 to 7, as said below
- swap_approval_flags: int32 [16], P('groups'), parts along dimension 0, may hold values from 0 to 1, as said below
- initial_signal_projector: bfloat16 [128, 128], replicated, may hold values from -0.5 to 0.5
- initial_distance_filter: float32 [8, 128], replicated, may hold values from -2 to 2
- initial_directional_scales: float32 [128], replicated, may hold values from 0.5 to 1.5
- invariant_revision_matrix: bfloat16 [128, 128], replicated, may hold values from -0.5 to 0.5
- magnitude_revision_matrix: bfloat16 [128, 128], replicated, may hold values from -0.5 to 0.5
- later_signal_projector: bfloat16 [128, 128], replicated, may hold values from -0.5 to 0.5
- later_directional_scales: float32 [128], replicated, may hold values from 0.5 to 1.5
- push_output_matrix: float32 [128], replicated, may hold values from -0.5 to 0.5
Outputs:
- positions_new: float32 [16, 3, 3072], P('groups', None, 'dom'), parts along dimension 0
- velocities_new: float32 [16, 3, 3072], P('groups', None, 'dom'), parts along dimension 0
- forces_new: float32 [16, 3, 3072], P('groups', None, 'dom'), parts along dimension 0
The draws below stay inside these ranges and needn't reach their ends.
There are 2 independent parts, one for each index of `groups`. The reference program is written for one: setup_inputs(seed, part) draws one part's arguments, and reference() takes and returns one part's arrays. A program takes and returns all parts, laid end to end along the dimension named above; an argument that names none is the same for every part. Nothing has to cross between parts.
Inputs may be any that keep to these rules, and one draw needn't show every extreme that they name: `particle_places`: the atoms of cell k have x and y in [0, 1) and z in [k, k + 1). `swap_counterpart_slot`: an involution that pairs neighbouring replicas, either (0, 1), (2, 3), ... or (1, 2), (3, 4), ..., a replica left without a pair being its own partner. `swap_approval_flags`: equal for the two replicas of a pair, 0 for a replica that is its own partner.
All inputs are finite; a program needn't handle non-finite values.
Results may differ from the reference program's by a relative error of at most 0.012.
The reference program's roundings to bfloat16 on the way count: a program that leaves them out, or rounds other values in their place, can miss the bound.
Values may be sent and summed in bfloat16 or wider, within the bound.
A program may use at most 64 MiB of HBM per device.

```python
import math
import jax
import jax.numpy as jnp
from jax import lax

LADDER_RUNGS = 8
NA = 64
HC = 1
F = 128
K = 8
STEPS = 4
NC = 48
ATOMS = 3072


def draw_particle_places(key, part):
    spread = jax.random.uniform(jax.random.fold_in(key, 3), (LADDER_RUNGS, 3, ATOMS), jnp.float32)
    cell_rows = (jnp.arange(ATOMS) // NA).astype(jnp.float32)
    lifted = jnp.array([0.0, 0.0, 1.0], jnp.float32)[None, :, None] * cell_rows[None, None, :]
    return spread + lifted


def draw_particle_speeds(key, part):
    cell_frac = (jnp.arange(ATOMS) // NA).astype(jnp.float32) / NC
    drawn_base = jnp.clip(jax.random.normal(jax.random.fold_in(key, 5), (LADDER_RUNGS, 3, ATOMS), jnp.float32), -4.0, 4.0)
    return drawn_base * jnp.sqrt(1.0 + 2.0 * cell_frac)[None, None, :]


def swap_table(key, part):
    coin_parity = jax.random.randint(jax.random.fold_in(key, 7), (), 0, 2)
    parity = (coin_parity + jnp.asarray(part, jnp.int32)) % 2
    ladder_slot = jnp.arange(LADDER_RUNGS)
    paired = ladder_slot + 1 - 2 * ((ladder_slot + parity) % 2)
    exchange_mate = jnp.where((paired < 0) | (paired >= LADDER_RUNGS), ladder_slot, paired)
    coin_flips = jax.random.randint(jax.random.fold_in(key, 11), (LADDER_RUNGS,), 0, 2)
    coin_flips = jnp.where(ladder_slot == parity, 1, coin_flips)
    coin_flips = jnp.where(ladder_slot == LADDER_RUNGS - 2 - parity, 0, coin_flips)
    low_index = jnp.minimum(ladder_slot, exchange_mate)
    accepted = coin_flips[low_index]
    accepted = jnp.where(exchange_mate == ladder_slot, 0, accepted)
    return (exchange_mate.astype(jnp.int32), accepted.astype(jnp.int32))


def draw_swap_counterpart_slot(key, part):
    return swap_table(key, part)[0]


def draw_swap_approval_flags(key, part):
    return swap_table(key, part)[1]


def shard_levels(own_key, extent, cuts, least, largest):
    def one(position, blocks):
        draws = jax.random.uniform(jax.random.fold_in(jax.random.fold_in(own_key, 6), position), (blocks,), jnp.float32, least / len(cuts), largest / len(cuts))
        return jnp.repeat(jnp.exp(draws), extent[position] // blocks).reshape((-1,) + (1,) * (len(extent) - position - 1))

    factor_of = one(*cuts[0])
    for cut in cuts[1:]:
        factor_of = factor_of * one(*cut)
    return factor_of


def bell_draw(own_key, dims, width, reach, pieces=(), kind=jnp.bfloat16):
    values = jax.random.normal(own_key, dims, jnp.float32) * width
    if len(pieces) > 0:
        values = shard_levels(own_key, dims, pieces, -0.22, 0.18) * values
    return jnp.clip(values, min=-reach, max=reach).astype(kind)


def setup_inputs(seed: int = 0, part: int = 0) -> dict:
    key_of = jax.random.split(jax.random.key(seed), 15)
    part_splits = jax.random.split(jax.random.fold_in(key_of[14], part), 15)
    particle_places = draw_particle_places(jax.random.fold_in(jax.random.fold_in(key_of[14], part), 71), part)
    particle_speeds = draw_particle_speeds(jax.random.fold_in(jax.random.fold_in(key_of[14], part), 71), part)
    thermal_targets = jnp.clip(jnp.exp(jax.random.uniform(part_splits[2], (LADDER_RUNGS,), jnp.float32, math.log(0.5), math.log(2.0))), 0.5, 2.0)
    element_features = bell_draw(part_splits[3], (ATOMS, F), 1.0, 4.0, ((0, 16),))
    swap_counterpart_slot = draw_swap_counterpart_slot(jax.random.fold_in(jax.random.fold_in(key_of[14], part), 71), part)
    swap_approval_flags = draw_swap_approval_flags(jax.random.fold_in(jax.random.fold_in(key_of[14], part), 71), part)
    initial_signal_projector = bell_draw(key_of[6], (F, F), F ** -0.5, 0.5)
    initial_distance_filter = bell_draw(key_of[7], (K, F), K ** -0.5, 2.0, (), jnp.float32)
    initial_directional_scales = jnp.clip(jax.random.uniform(key_of[8], (F,), jnp.float32, 0.5, 1.5), 0.5, 1.5)
    invariant_revision_matrix = bell_draw(key_of[9], (F, F), F ** -0.5, 0.5)
    magnitude_revision_matrix = bell_draw(key_of[10], (F, F), F ** -0.5, 0.5)
    later_signal_projector = bell_draw(key_of[11], (F, F), F ** -0.5, 0.5)
    later_directional_scales = jnp.clip(jax.random.uniform(key_of[12], (F,), jnp.float32, 0.5, 1.5), 0.5, 1.5)
    push_output_matrix = bell_draw(key_of[13], (F,), F ** -0.5, 0.5, (), jnp.float32)
    return dict(particle_places=particle_places, particle_speeds=particle_speeds, thermal_targets=thermal_targets, element_features=element_features, swap_counterpart_slot=swap_counterpart_slot, swap_approval_flags=swap_approval_flags, initial_signal_projector=initial_signal_projector, initial_distance_filter=initial_distance_filter, initial_directional_scales=initial_directional_scales, invariant_revision_matrix=invariant_revision_matrix, magnitude_revision_matrix=magnitude_revision_matrix, later_signal_projector=later_signal_projector, later_directional_scales=later_directional_scales, push_output_matrix=push_output_matrix)


step_time = 0.05
motion_work_lower_limit = 1e-06

def radial_rows(own_coords, part_coords, basis_count):
    displacement = part_coords[:, :, :, None, :] - own_coords[:, :, :, :, None]
    squared = lax.optimization_barrier(jnp.sum(displacement * displacement, axis=1))
    envelope = jnp.where(squared < 1.0, (1.0 - squared) * (1.0 - squared), 0.0)
    vectors = jnp.moveaxis(displacement * envelope[:, None], 1, 3)
    if basis_count == 0:
        return vectors.astype(jnp.bfloat16)
    centers = jnp.arange(basis_count, dtype=jnp.float32) / (basis_count - 1)
    sharpness = 2.0 * (basis_count - 1) * (basis_count - 1)
    offset = squared[:, :, :, None, :] - centers[:, None]
    gaussians = jnp.exp(-sharpness * offset * offset) * envelope[:, :, :, None, :]
    return jnp.concatenate([gaussians, vectors], axis=3).astype(jnp.bfloat16)

def periodic_pad(source_array, width_atoms, along_axis):
    length = source_array.shape[along_axis]
    head_part = lax.slice_in_dim(source_array, length - width_atoms, length, axis=along_axis)
    tail_part = lax.slice_in_dim(source_array, 0, width_atoms, axis=along_axis)
    return jnp.concatenate([head_part, source_array, tail_part], axis=along_axis)

def force_field(location_triples, element_features, first_table, initial_distance_filter, initial_directional_scales, invariant_revision_matrix, magnitude_revision_matrix, later_signal_projector, later_directional_scales, push_output_matrix):
    replicas = location_triples.shape[0]
    cell_total = location_triples.shape[2] // NA
    channels = invariant_revision_matrix.shape[0]
    basis_count = initial_distance_filter.shape[0]
    reach_atoms = (2 * HC + 1) * NA
    padded = periodic_pad(location_triples, HC * NA, 2)
    cell_number = jnp.arange(padded.shape[2], dtype=jnp.int32) // NA - HC
    wrap_shift = (jnp.where(cell_number < 0, -1.0, 0.0) + jnp.where(cell_number >= cell_total, 1.0, 0.0)) * cell_total
    axis_mask = jnp.array([0.0, 0.0, 1.0], jnp.float32)
    near_coords = padded + axis_mask[None, :, None] * wrap_shift[None, None, :]

    def windows(cell_index):
        own_coords = lax.dynamic_slice_in_dim(near_coords, (cell_index + HC) * NA, NA, 2)
        part_coords = lax.dynamic_slice_in_dim(near_coords, cell_index * NA, reach_atoms, 2)
        return (own_coords[:, :, None], part_coords[:, :, None])

    def layer_one(cell_index):
        own_coords, part_coords = windows(cell_index)
        single_row_count = lax.optimization_barrier(radial_rows(own_coords, part_coords, basis_count)).astype(jnp.float32)
        exchange_mate = lax.dynamic_slice_in_dim(first_table, cell_index * NA, reach_atoms, 0).astype(jnp.float32)
        reduced_sum = jnp.einsum('rcaxb,bf->rcaxf', single_row_count, exchange_mate, precision=lax.Precision.HIGHEST)[:, 0]
        scalar = lax.optimization_barrier(jnp.sum(reduced_sum[:, :, :basis_count] * initial_distance_filter, axis=2))
        vector_one = reduced_sum[:, :, basis_count:] * initial_directional_scales
        norm_square = lax.optimization_barrier(jnp.sum(vector_one * vector_one, axis=2))
        update = jnp.dot(scalar.astype(jnp.bfloat16).reshape(-1, channels), invariant_revision_matrix, preferred_element_type=jnp.float32)
        update = update + jnp.dot(norm_square.astype(jnp.bfloat16).reshape(-1, channels), magnitude_revision_matrix, preferred_element_type=jnp.float32)
        self_rows = lax.dynamic_slice_in_dim(element_features, cell_index * NA, NA, 0).astype(jnp.float32)
        hidden = (self_rows[None] + jax.nn.silu(update).reshape(replicas, NA, channels)).astype(jnp.bfloat16)
        return (hidden, vector_one)
    cell_list = jnp.arange(cell_total, dtype=jnp.int32)
    hidden_all, vector_all = lax.map(layer_one, cell_list)
    hidden_rows = jnp.moveaxis(hidden_all, 0, 1).reshape(replicas * cell_total * NA, channels)
    second = jnp.dot(hidden_rows, later_signal_projector, preferred_element_type=jnp.float32).astype(jnp.bfloat16)
    second_table = periodic_pad(second.reshape(replicas, cell_total * NA, channels), HC * NA, 1)

    def layer_two(cell_index):
        own_coords, part_coords = windows(cell_index)
        rows_two = lax.optimization_barrier(radial_rows(own_coords, part_coords, 0)).astype(jnp.float32)
        exchange_mate = lax.dynamic_slice_in_dim(second_table, cell_index * NA, reach_atoms, 1).astype(jnp.float32)
        reduced_sum = jnp.einsum('rcaxb,rbf->rcaxf', rows_two, exchange_mate, precision=lax.Precision.HIGHEST)[:, 0]
        total = vector_all[cell_index] + reduced_sum * later_directional_scales
        return lax.optimization_barrier(jnp.sum(total * push_output_matrix, axis=3))
    force_cells = lax.map(layer_two, cell_list)
    return jnp.transpose(force_cells, (1, 3, 0, 2)).reshape(replicas, 3, cell_total * NA)

def reference(particle_places, particle_speeds, thermal_targets, element_features, swap_counterpart_slot, swap_approval_flags, initial_signal_projector, initial_distance_filter, initial_directional_scales, invariant_revision_matrix, magnitude_revision_matrix, later_signal_projector, later_directional_scales, push_output_matrix):
    particle_number_overall = particle_places.shape[2]
    first_table = periodic_pad(jnp.dot(element_features, initial_signal_projector, preferred_element_type=jnp.float32).astype(jnp.bfloat16), HC * NA, 0)

    def evaluate(location_triples):
        return force_field(location_triples, element_features, first_table, initial_distance_filter, initial_directional_scales, invariant_revision_matrix, magnitude_revision_matrix, later_signal_projector, later_directional_scales, push_output_matrix)
    location_triples = particle_places
    speed_entry = particle_speeds
    present_push = evaluate(location_triples)
    for step_index in range(STEPS):
        half_velocity = speed_entry + 0.5 * step_time * present_push
        location_triples = location_triples + step_time * half_velocity
        present_push = evaluate(location_triples)
        speed_entry = half_velocity + 0.5 * step_time * present_push
        motion_work_amount = lax.optimization_barrier(jnp.sum(speed_entry * speed_entry, axis=(1, 2)))
        stretch_multiplier = jnp.sqrt(thermal_targets / (motion_work_amount / (3.0 * particle_number_overall) + motion_work_lower_limit))
        speed_entry = speed_entry * stretch_multiplier[:, None, None]
    ladder_slot = jnp.arange(thermal_targets.shape[0], dtype=jnp.int32)
    source = jnp.where(swap_approval_flags > 0, swap_counterpart_slot, ladder_slot)
    selected_entries = (source[:, None] == ladder_slot[None, :]).astype(jnp.float32)

    def select_entries(values):
        return lax.optimization_barrier(jnp.sum(selected_entries[:, :, None, None] * values[None], axis=1))
    thermal_ratio = jnp.sqrt(thermal_targets / lax.optimization_barrier(jnp.sum(selected_entries * thermal_targets[None, :], axis=1)))
    atom_cell = (jnp.arange(particle_number_overall, dtype=jnp.int32) // NA).astype(jnp.float32)
    cell_floor = jnp.array([0.0, 0.0, 1.0], jnp.float32)[:, None] * atom_cell[None, :]
    return (select_entries(location_triples) - cell_floor[None], select_entries(speed_entry) * thermal_ratio[:, None, None], select_entries(present_push))
```

```python
import functools
import math

import jax
import jax.numpy as jnp
from jax import lax
from jax.experimental import pallas as pl
from jax.experimental.pallas import tpu as pltpu
from jax.sharding import PartitionSpec as P

NA = 64
STEPS = 4
LANES = 128
CHUNK = 32

step_time = 0.05
motion_work_lower_limit = 1e-06

F32 = jnp.float32
BF16 = jnp.bfloat16
MESH = pl.DeviceIdType.MESH
NT = (((1,), (1,)), ((), ()))


def split_bf16(values):
    high = values.astype(BF16)
    low = (values - high.astype(F32)).astype(BF16)
    return high, low


def weight_rows(weights):
    high, low = split_bf16(weights)
    high, low = high.astype(F32), low.astype(F32)
    row = lax.broadcasted_iota(jnp.int32, (16, weights.shape[1]), 0)
    return jnp.where(row == 0, high, jnp.where(row == 1, low, 0.0)).astype(BF16)


def pair_base(rows, columns):
    dx, dy, dz = [row - column for row, column in zip(rows, columns)]
    squared = dx * dx + dy * dy + dz * dz
    inside = jnp.maximum(1.0 - squared, 0.0)
    envelope = inside * inside
    centered = jnp.minimum(squared, 1.0) - 0.5
    return (dx * envelope, dy * envelope, dz * envelope), envelope, centered


def kernel(
    n, replicas, cells, group,
    places, speeds, targets, slots, flags, features,
    projector, radial_filter, scales_one, invariant, magnitude, later_projector, scales_two, push,
    places_out, speeds_out, forces_out,
    feature_halo, place_send, place_halo, table_one, table_vec, s_one,
    state_x, state_v, state_g, win, columns, gauss, vectors, s_own,
    s_send, s_recv, vg_send, vg_recv, kin_send, kin_recv,
    init_send_sem, init_recv_sem, s_send_sem, s_recv_sem, vg_send_sem, vg_recv_sem,
    kin_send_sem, kin_recv_sem,
):
    me = lax.axis_index("dom")
    left = lax.rem(me + n - 1, n)
    right = lax.rem(me + 1, n)
    own = cells * NA
    width = state_x.shape[2]
    right_at, left_at = own, own + NA
    channels = features.shape[1]

    def cell_at(c):
        return left_at if c < 0 else c * NA

    barrier = pltpu.get_barrier_semaphore()

    def greet(d, carry):
        pl.semaphore_signal(barrier, inc=1, device_id={"dom": lax.rem(me + d, n)}, device_id_type=MESH)
        return carry

    lax.fori_loop(1, n, greet, 0)

    zeros_pad = jnp.zeros((replicas, width - own), F32)
    for c in range(3):
        x = places[:, c, :]
        place_send[c] = jnp.concatenate([x[:, :NA], x[:, own - NA:]], axis=1)
        state_x[c, :, :] = jnp.concatenate([x, zeros_pad], axis=1)
        state_v[c, :, :] = jnp.concatenate([speeds[:, c, :], zeros_pad], axis=1)
        state_g[c, :, :] = jnp.zeros((replicas, width), F32)

    pl.semaphore_wait(barrier, n - 1)

    def remote(src, dst, send_sem, recv_sem, to):
        return pltpu.make_async_remote_copy(
            src_ref=src, dst_ref=dst, send_sem=send_sem, recv_sem=recv_sem,
            device_id={"dom": to}, device_id_type=MESH,
        )

    first = [
        remote(place_send, place_halo.at[1], init_send_sem.at[0], init_recv_sem.at[0], left),
        remote(place_send, place_halo.at[0], init_send_sem.at[1], init_recv_sem.at[1], right),
        remote(features.at[pl.ds(0, NA)], feature_halo.at[1], init_send_sem.at[2], init_recv_sem.at[2], left),
        remote(features.at[pl.ds(own - NA, NA)], feature_halo.at[0], init_send_sem.at[3], init_recv_sem.at[3], right),
    ]
    for copy in first:
        copy.start()

    filters = radial_filter[...]
    push_row = push[...]
    w_one = weight_rows(scales_one[...] * push_row)
    w_two = weight_rows(scales_two[...] * push_row)
    scale_row = scales_one[...]

    def make_table(rows):
        return jnp.dot(rows, projector[...], preferred_element_type=F32).astype(BF16)

    tables = {c: make_table(features[c * NA:(c + 1) * NA, :]) for c in range(cells)}
    for copy in first:
        copy.wait()
    tables[-1] = make_table(feature_halo[0])
    tables[cells] = make_table(feature_halo[1])

    s_parts = []
    for c in list(range(cells)) + [cells, -1]:
        out = lax.dot_general(w_one, tables[c], NT, preferred_element_type=F32)
        s_parts.append(out[0:1] + out[1:2])
    s_one[...] = jnp.concatenate(s_parts + [jnp.zeros((1, width - own - 2 * NA), F32)], axis=1)

    for c in range(cells):
        before, here, after = [tables[c + j].astype(F32) for j in (-1, 0, 1)]
        table_vec[c, 0:NA, :] = tables[c - 1]
        table_vec[c, NA:2 * NA, :] = tables[c]
        table_vec[c, 2 * NA:3 * NA, :] = tables[c + 1]
        table_vec[c, 3 * NA:4 * NA, :] = jnp.zeros((NA, channels), BF16)
        for k in range(8):
            row = filters[k:k + 1]
            table_one[c, k * LANES:k * LANES + NA, :] = (before * row).astype(BF16)
            table_one[c, k * LANES + NA:(k + 1) * LANES, :] = (here * row).astype(BF16)
        for j in range(4):
            at = (8 + j) * LANES
            table_one[c, at:at + NA, :] = (after * filters[4 + j:5 + j]).astype(BF16)
            table_one[c, at + NA:at + LANES, :] = (after * filters[3 - j:4 - j]).astype(BF16)

    for c in range(3):
        state_x[c, :, right_at:right_at + NA] = place_halo[1, c, :, 0:NA]
        state_x[c, :, left_at:left_at + NA] = place_halo[0, c, :, NA:2 * NA]

    total = float(cells * n)
    lane = lax.broadcasted_iota(jnp.int32, (1, width), 1)
    up = jnp.where(me == n - 1, total, 0.0).astype(F32)
    down = jnp.where(me == 0, -total, 0.0).astype(F32)
    shift = jnp.where(
        (lane >= right_at) & (lane < right_at + NA), up,
        jnp.where((lane >= left_at) & (lane < left_at + NA), down, 0.0),
    )
    side = jnp.where(lax.broadcasted_iota(jnp.int32, (1, LANES), 1) < NA, 14.0, -14.0).astype(F32)
    replica_row = lax.broadcasted_iota(jnp.int32, (replicas, 1), 0)
    diagonal = (
        lax.broadcasted_iota(jnp.int32, (replicas, LANES), 0)
        == lax.broadcasted_iota(jnp.int32, (replicas, LANES), 1)
    )
    target = jnp.zeros((replicas, 1), F32)
    source = jnp.zeros((replicas, 1), jnp.int32)
    for r in range(replicas):
        target = jnp.where(replica_row == r, targets[r], target)
        source = jnp.where(replica_row == r, jnp.where(flags[r] > 0, slots[r], r), source)

    ratio = math.exp(-4.0)

    def chain(start, power):
        values = [start]
        for _ in range(3):
            values.append(values[-1] * power)
            power = power * ratio
        return values

    def build(c, r, slot):
        rows = [win[c, d, r:r + 1, :] for d in range(3)]
        for at in range(0, NA, CHUNK):
            here = slice(at, at + CHUNK)
            cols = [
                columns[c * NA + at:c * NA + at + CHUNK, d * replicas + r:d * replicas + r + 1]
                for d in range(3)
            ]
            cols = [jnp.broadcast_to(col, (CHUNK, LANES)) for col in cols]
            vec, envelope, t = pair_base([row[:, :LANES] for row in rows], cols)
            for d in range(3):
                vectors[c, r, d * NA + at:d * NA + at + CHUNK, 0:LANES] = vec[d].astype(BF16)
            base = jnp.exp(-98.0 * (t * t) - 0.5) * envelope
            grow = jnp.exp(14.0 * t)
            shrink = jnp.exp(-14.0 * t)
            high = chain(base * grow, grow * grow * ratio)
            low = chain(base * shrink, shrink * shrink * ratio)
            out = slice(slot * NA + at, slot * NA + at + CHUNK)
            for j in range(4):
                gauss[out, (4 + j) * LANES:(5 + j) * LANES] = high[j].astype(BF16)
                gauss[out, (3 - j) * LANES:(4 - j) * LANES] = low[j].astype(BF16)
            vec, envelope, t = pair_base([row[:, LANES:] for row in rows], cols)
            for d in range(3):
                vectors[c, r, d * NA + at:d * NA + at + CHUNK, LANES:] = vec[d].astype(BF16)
            base = jnp.exp(-98.0 * (t * t) - 0.5) * envelope
            grow = jnp.exp(side * t)
            both = chain(base * grow, grow * grow * ratio)
            for j in range(4):
                gauss[out, (8 + j) * LANES:(9 + j) * LANES] = both[j].astype(BF16)

    def layer_one(c, part):
        members = range(part * group, (part + 1) * group)
        base = part * group * NA
        for r in members:
            build(c, r, r)
        scalar = jnp.dot(
            gauss[base:base + group * NA, :], table_one[c], preferred_element_type=F32
        ).astype(BF16)
        norms = []
        for r in members:
            vec = jnp.dot(vectors[c, r], table_vec[c], preferred_element_type=F32)
            square = 0.0
            for d in range(3):
                one = vec[d * NA:(d + 1) * NA] * scale_row
                square = square + one * one
            norms.append(square.astype(BF16))
        norm = jnp.concatenate(norms, axis=0)
        update = jnp.dot(scalar, invariant[...], preferred_element_type=F32)
        update = update + jnp.dot(norm, magnitude[...], preferred_element_type=F32)
        own_rows = features[c * NA:(c + 1) * NA, :].astype(F32)
        hidden = update / (1.0 + jnp.exp(-update)) + jnp.concatenate([own_rows] * group, axis=0)
        second = jnp.dot(
            hidden.astype(BF16), later_projector[...], preferred_element_type=F32
        ).astype(BF16)
        out = lax.dot_general(w_two, second, NT, preferred_element_type=F32)
        flat = out[0:1] + out[1:2]
        return [flat[:, i * NA:(i + 1) * NA] for i in range(group)]

    def cell_sources(c):
        rows = []
        for part in range(replicas // group):
            rows.extend(layer_one(c, part))
        return jnp.concatenate(rows, axis=0) + s_one[0:1, c * NA:(c + 1) * NA]

    def force(c, before, here, after):
        window = jnp.concatenate([before, here, after, jnp.zeros_like(after)], axis=1)
        high, low = split_bf16(window)
        stacked = jnp.concatenate([high.astype(F32), low.astype(F32)], axis=0).astype(BF16)
        result = jnp.zeros((replicas, 3 * NA), F32)
        for r in range(replicas):
            out = lax.dot_general(stacked, vectors[c, r], NT, preferred_element_type=F32)
            result = jnp.where(replica_row == r, out[:replicas] + out[replicas:], result)
        return result

    order = [0] if cells == 1 else [0, cells - 1] + list(range(1, cells - 1))

    def step(t, carry):
        moving = jnp.where(t > 0, 1.0, 0.0).astype(F32)
        places_now, half_speeds = [], []
        for d in range(3):
            half = state_v[d] + (0.5 * step_time) * state_g[d]
            x = state_x[d] + (moving * step_time) * half
            state_x[d] = x
            half_speeds.append(half[:, :own])
            if d == 2:
                x = x + shift
            places_now.append(x)
        for c in range(cells):
            for d in range(3):
                x = places_now[d]
                pieces = [x[:, at:at + NA] for at in (cell_at(c - 1), cell_at(c), cell_at(c + 1))]
                win[c, d, :, :] = jnp.concatenate(pieces + pieces[2:], axis=1)
        tall = jnp.concatenate(places_now, axis=0)
        for at in range(0, own, LANES):
            columns[at:at + LANES, 0:3 * replicas] = tall[:, at:at + LANES].T

        sources = {}
        sent = []

        def send_sources():
            s_send[t] = jnp.concatenate([sources[0], sources[cells - 1]], axis=1)
            sent.append(remote(s_send.at[t], s_recv.at[t, 1], s_send_sem.at[t, 0], s_recv_sem.at[t, 0], left))
            sent.append(remote(s_send.at[t], s_recv.at[t, 0], s_send_sem.at[t, 1], s_recv_sem.at[t, 1], right))
            for copy in sent:
                copy.start()

        for c in order:
            sources[c] = cell_sources(c)
            if not sent and 0 in sources and cells - 1 in sources:
                send_sources()
        forces = {}
        for c in order[2:]:
            forces[c] = force(c, sources[c - 1], sources[c], sources[c + 1])
        for copy in sent:
            copy.wait()
        sources[-1] = s_recv[t, 0, :, NA:2 * NA]
        sources[cells] = s_recv[t, 1, :, 0:NA]
        for c in order[:2]:
            forces[c] = force(c, sources[c - 1], sources[c], sources[c + 1])

        kinetic = jnp.zeros((replicas, 1), F32)
        pushes, quick = [], []
        for d in range(3):
            g = jnp.concatenate([forces[c][:, d * NA:(d + 1) * NA] for c in range(cells)], axis=1)
            v = half_speeds[d] + (moving * (0.5 * step_time)) * g
            vg_send[t, 0, d, :, :] = jnp.concatenate([v[:, :NA], g[:, :NA]], axis=1)
            vg_send[t, 1, d, :, :] = jnp.concatenate([v[:, own - NA:], g[:, own - NA:]], axis=1)
            kinetic = kinetic + jnp.sum(v * v, axis=1, keepdims=True)
            pushes.append(g)
            quick.append(v)
        across = jnp.sum(jnp.where(diagonal, kinetic, 0.0), axis=0, keepdims=True)
        kin_send[t] = across
        kin_recv[t, n - 1] = across

        def spread(d, inner):
            remote(
                kin_send.at[t], kin_recv.at[t, d - 1], kin_send_sem.at[t], kin_recv_sem.at[t],
                lax.rem(me + d, n),
            ).start()
            return inner

        lax.fori_loop(1, n, spread, 0)
        swaps = [
            remote(vg_send.at[t, 0], vg_recv.at[t, 1], vg_send_sem.at[t, 0], vg_recv_sem.at[t, 0], left),
            remote(vg_send.at[t, 1], vg_recv.at[t, 0], vg_send_sem.at[t, 1], vg_recv_sem.at[t, 1], right),
        ]
        for copy in swaps:
            copy.start()
        everything = kin_recv.at[t, pl.ds(0, n - 1)]
        pltpu.make_async_copy(everything, everything, kin_send_sem.at[t]).wait()
        pltpu.make_async_copy(everything, everything, kin_recv_sem.at[t]).wait()
        for copy in swaps:
            copy.wait()
        collected = jnp.sum(kin_recv[t], axis=0)
        gathered = jnp.sum(
            jnp.where(diagonal, collected, 0.0), axis=1, keepdims=True
        )
        stretch = jnp.sqrt(target / (gathered / (3.0 * own * n) + motion_work_lower_limit))
        stretch = jnp.where(t > 0, stretch, 1.0)
        rest = jnp.zeros((replicas, width - own - 2 * NA), F32)
        for d in range(3):
            from_left, from_right = vg_recv[t, 0, d], vg_recv[t, 1, d]
            state_v[d] = stretch * jnp.concatenate(
                [quick[d], from_right[:, :NA], from_left[:, :NA], rest], axis=1
            )
            state_g[d] = jnp.concatenate(
                [pushes[d], from_right[:, NA:], from_left[:, NA:], rest], axis=1
            )
        return carry

    lax.fori_loop(0, STEPS + 1, step, 0)

    def pick(values):
        result = jnp.zeros_like(values)
        for r in range(replicas):
            result = jnp.where(source == r, values[r:r + 1], result)
        return result

    heat = jnp.sqrt(target / pick(target))
    floor = (
        me * cells + lax.broadcasted_iota(jnp.int32, (1, own), 1) // NA
    ).astype(F32)
    for d in range(3):
        x = pick(state_x[d][:, :own])
        if d == 2:
            x = x - floor
        places_out[:, d, :] = x
        speeds_out[:, d, :] = pick(state_v[d][:, :own]) * heat
        forces_out[:, d, :] = pick(state_g[d][:, :own])


def on_device(
    particle_places,
    particle_speeds,
    thermal_targets,
    element_features,
    swap_counterpart_slot,
    swap_approval_flags,
    initial_signal_projector,
    initial_distance_filter,
    initial_directional_scales,
    invariant_revision_matrix,
    magnitude_revision_matrix,
    later_signal_projector,
    later_directional_scales,
    push_output_matrix,
):
    n = lax.axis_size("dom")
    replicas, _, own = particle_places.shape
    cells = own // NA
    channels = element_features.shape[1]
    width = -(-(own + 2 * NA) // LANES) * LANES
    padded = -(-own // LANES) * LANES
    rounds = STEPS + 1
    group = min(4, replicas)
    basis = initial_distance_filter.shape[0]
    depth = basis * 3 * NA
    vmem = pl.BlockSpec(memory_space=pltpu.VMEM)
    smem = pl.BlockSpec(memory_space=pltpu.SMEM)
    out = jax.ShapeDtypeStruct(particle_places.shape, F32)
    return pl.pallas_call(
        functools.partial(kernel, n, replicas, cells, group),
        out_shape=(out, out, out),
        in_specs=[vmem, vmem, smem, smem, smem] + [vmem] * 9,
        out_specs=(vmem, vmem, vmem),
        scratch_shapes=[
            pltpu.VMEM((2, NA, channels), BF16),
            pltpu.VMEM((3, replicas, LANES), F32),
            pltpu.VMEM((2, 3, replicas, LANES), F32),
            pltpu.VMEM((cells, depth, channels), BF16),
            pltpu.VMEM((cells, 4 * NA, channels), BF16),
            pltpu.VMEM((1, width), F32),
            pltpu.VMEM((3, replicas, width), F32),
            pltpu.VMEM((3, replicas, width), F32),
            pltpu.VMEM((3, replicas, width), F32),
            pltpu.VMEM((cells, 3, replicas, 2 * LANES), F32),
            pltpu.VMEM((padded, 3 * replicas), F32),
            pltpu.VMEM((replicas * NA, depth), BF16),
            pltpu.VMEM((cells, replicas, 3 * NA, 2 * LANES), BF16),
            pltpu.VMEM((replicas, width), F32),
            pltpu.VMEM((rounds, replicas, LANES), F32),
            pltpu.VMEM((rounds, 2, replicas, LANES), F32),
            pltpu.VMEM((rounds, 2, 3, replicas, LANES), F32),
            pltpu.VMEM((rounds, 2, 3, replicas, LANES), F32),
            pltpu.VMEM((rounds, 1, LANES), F32),
            pltpu.VMEM((rounds, n, 1, LANES), F32),
            pltpu.SemaphoreType.DMA((4,)),
            pltpu.SemaphoreType.DMA((4,)),
            pltpu.SemaphoreType.DMA((rounds, 2)),
            pltpu.SemaphoreType.DMA((rounds, 2)),
            pltpu.SemaphoreType.DMA((rounds, 2)),
            pltpu.SemaphoreType.DMA((rounds, 2)),
            pltpu.SemaphoreType.DMA((rounds,)),
            pltpu.SemaphoreType.DMA((rounds,)),
        ],
        compiler_params=pltpu.CompilerParams(
            collective_id=0, has_side_effects=True, vmem_limit_bytes=48 * 1024 * 1024
        ),
    )(
        particle_places,
        particle_speeds,
        thermal_targets,
        swap_counterpart_slot,
        swap_approval_flags,
        element_features,
        initial_signal_projector,
        initial_distance_filter,
        initial_directional_scales.reshape(1, -1),
        invariant_revision_matrix,
        magnitude_revision_matrix,
        later_signal_projector,
        later_directional_scales.reshape(1, -1),
        push_output_matrix.reshape(1, -1),
    )


def solution(mesh):
    along = P("groups", None, "dom")
    return jax.shard_map(
        on_device,
        mesh=mesh,
        in_specs=(
            along,
            along,
            P("groups"),
            P(("groups", "dom"), None),
            P("groups"),
            P("groups"),
            P(),
            P(),
            P(),
            P(),
            P(),
            P(),
            P(),
            P(),
        ),
        out_specs=(along, along, along),
        check_vma=False,
    )
```

```python
import functools
import math

import jax
import jax.numpy as jnp
from jax import lax
from jax.experimental import pallas as pl
from jax.experimental.pallas import tpu as pltpu
from jax.sharding import PartitionSpec as P

NA = 64
STEPS = 4
LANES = 128
CHUNK = 16
LOG2E = math.log2(math.e)

step_time = 0.05
motion_work_lower_limit = 1e-06

F32 = jnp.float32
BF16 = jnp.bfloat16
MESH = pl.DeviceIdType.MESH
NT = (((1,), (1,)), ((), ()))


def split_bf16(values):
    high = values.astype(BF16)
    low = (values - high.astype(F32)).astype(BF16)
    return high, low


def weight_rows(weights):
    high, low = split_bf16(weights)
    high, low = high.astype(F32), low.astype(F32)
    row = lax.broadcasted_iota(jnp.int32, (16, weights.shape[1]), 0)
    return jnp.where(row == 0, high, jnp.where(row == 1, low, 0.0)).astype(BF16)


def pair_base(rows, columns):
    dx, dy, dz = [row - column for row, column in zip(rows, columns)]
    squared = dx * dx + dy * dy + dz * dz
    inside = jnp.maximum(1.0 - squared, 0.0)
    envelope = inside * inside
    centered = 0.5 - inside
    base = jnp.exp2((centered * centered) * (-98.0 * LOG2E)) * envelope
    return (dx * envelope, dy * envelope, dz * envelope), base, centered


def kernel(
    n, replicas, cells, parts,
    places, speeds, targets, slots, flags, features,
    projector, radial_filter, scales_one, invariant, magnitude, later_projector, scales_two, push,
    places_out, speeds_out, forces_out,
    feature_halo, place_send, place_halo, table_one, table_vec, s_one,
    state_x, state_v, state_g, win, columns, vectors,
    s_send, s_recv, vg_send, vg_recv, kin_send, kin_recv,
    init_send_sem, init_recv_sem, s_send_sem, s_recv_sem, vg_send_sem, vg_recv_sem,
    kin_send_sem, kin_recv_sem,
):
    me = lax.axis_index("dom")
    left = lax.rem(me + n - 1, n)
    right = lax.rem(me + 1, n)
    own = cells * NA
    width = state_x.shape[3]
    group = replicas // parts
    right_at, left_at = own, own + NA
    channels = features.shape[1]

    def cell_at(c):
        return left_at if c < 0 else c * NA

    barrier = pltpu.get_barrier_semaphore()

    def greet(d, carry):
        pl.semaphore_signal(barrier, inc=1, device_id={"dom": lax.rem(me + d, n)}, device_id_type=MESH)
        return carry

    lax.fori_loop(1, n, greet, 0)

    zeros_pad = jnp.zeros((group, width - own), F32)
    for d in range(3):
        x = places[d]
        place_send[d] = jnp.concatenate([x[:, :NA], x[:, own - NA:]], axis=1)
        for p in range(parts):
            members = slice(p * group, (p + 1) * group)
            state_x[p, d] = jnp.concatenate([x[members], zeros_pad], axis=1)
            state_v[p, d] = jnp.concatenate([speeds[d, members, :], zeros_pad], axis=1)
            state_g[p, d] = jnp.zeros((group, width), F32)

    pl.semaphore_wait(barrier, n - 1)

    def remote(src, dst, send_sem, recv_sem, to):
        return pltpu.make_async_remote_copy(
            src_ref=src, dst_ref=dst, send_sem=send_sem, recv_sem=recv_sem,
            device_id={"dom": to}, device_id_type=MESH,
        )

    first = [
        remote(place_send, place_halo.at[1], init_send_sem.at[0], init_recv_sem.at[0], left),
        remote(place_send, place_halo.at[0], init_send_sem.at[1], init_recv_sem.at[1], right),
        remote(features.at[pl.ds(0, NA)], feature_halo.at[1], init_send_sem.at[2], init_recv_sem.at[2], left),
        remote(features.at[pl.ds(own - NA, NA)], feature_halo.at[0], init_send_sem.at[3], init_recv_sem.at[3], right),
    ]
    for copy in first:
        copy.start()

    basis = radial_filter.shape[0]
    offset = lax.broadcasted_iota(jnp.int32, radial_filter.shape, 0).astype(F32) - 0.5 * (basis - 1)
    filters = radial_filter[...] * jnp.exp(-2.0 * offset * offset)
    push_row = push[...]
    w_one = weight_rows(scales_one[...] * push_row)
    w_two = weight_rows(scales_two[...] * push_row)
    scale_row = scales_one[...] * scales_one[...]

    def make_table(rows):
        return jnp.dot(rows, projector[...], preferred_element_type=F32).astype(BF16)

    tables = {c: make_table(features[c * NA:(c + 1) * NA, :]) for c in range(cells)}
    for copy in first:
        copy.wait()
    tables[-1] = make_table(feature_halo[0])
    tables[cells] = make_table(feature_halo[1])

    s_parts = []
    for c in list(range(cells)) + [cells, -1]:
        out = lax.dot_general(w_one, tables[c], NT, preferred_element_type=F32)
        s_parts.append(out[0:1] + out[1:2])
    s_one[...] = jnp.concatenate(s_parts + [jnp.zeros((1, width - own - 2 * NA), F32)], axis=1)

    for c in range(cells):
        before, here, after = [tables[c + j].astype(F32) for j in (-1, 0, 1)]
        table_vec[c, 0:NA, :] = tables[c - 1]
        table_vec[c, NA:2 * NA, :] = tables[c]
        table_vec[c, 2 * NA:3 * NA, :] = tables[c + 1]
        table_vec[c, 3 * NA:4 * NA, :] = jnp.zeros((NA, channels), BF16)
        for k in range(8):
            row = filters[k:k + 1]
            table_one[c, k * LANES:k * LANES + NA, :] = (before * row).astype(BF16)
            table_one[c, k * LANES + NA:(k + 1) * LANES, :] = (here * row).astype(BF16)
        for j in range(4):
            at = (8 + j) * LANES
            table_one[c, at:at + NA, :] = (after * filters[4 + j:5 + j]).astype(BF16)
            table_one[c, at + NA:at + LANES, :] = (after * filters[3 - j:4 - j]).astype(BF16)

    for d in range(3):
        for p in range(parts):
            members = slice(p * group, (p + 1) * group)
            state_x[p, d, :, right_at:right_at + NA] = place_halo[1, d, members, 0:NA]
            state_x[p, d, :, left_at:left_at + NA] = place_halo[0, d, members, NA:2 * NA]

    total = float(cells * n)
    lane = lax.broadcasted_iota(jnp.int32, (1, width), 1)
    up = jnp.where(me == n - 1, total, 0.0).astype(F32)
    down = jnp.where(me == 0, -total, 0.0).astype(F32)
    shift = jnp.where(
        (lane >= right_at) & (lane < right_at + NA), up,
        jnp.where((lane >= left_at) & (lane < left_at + NA), down, 0.0),
    )
    side = jnp.where(lax.broadcasted_iota(jnp.int32, (1, LANES), 1) < NA, 14.0 * LOG2E, -14.0 * LOG2E).astype(F32)
    member_row = lax.broadcasted_iota(jnp.int32, (group, 1), 0)
    replica_row = lax.broadcasted_iota(jnp.int32, (replicas, 1), 0)
    diagonal = (
        lax.broadcasted_iota(jnp.int32, (group, LANES), 0)
        == lax.broadcasted_iota(jnp.int32, (group, LANES), 1)
    )
    target = jnp.zeros((replicas, 1), F32)
    source = jnp.zeros((replicas, 1), jnp.int32)
    for r in range(replicas):
        target = jnp.where(replica_row == r, targets[r], target)
        source = jnp.where(replica_row == r, jnp.where(flags[r] > 0, slots[r], r), source)

    def chain(start, power):
        values = [start]
        for _ in range(3):
            values.append(values[-1] * power)
        return values

    def build(p, c, r):
        rows = [win[p, c, d, r:r + 1, :] for d in range(3)]
        tall = []
        for at in range(0, NA, CHUNK):
            out = slice(at, at + CHUNK)
            cols = [
                columns[p, c * NA + at:c * NA + at + CHUNK, d * group + r:d * group + r + 1]
                for d in range(3)
            ]
            cols = [jnp.broadcast_to(col, (CHUNK, LANES)) for col in cols]
            vec, base, t = pair_base([row[:, :LANES] for row in rows], cols)
            for d in range(3):
                vectors[p, c, r, d * NA + at:d * NA + at + CHUNK, 0:LANES] = vec[d].astype(BF16)
            grow = jnp.exp2((14.0 * LOG2E) * t)
            shrink = jnp.exp2((-14.0 * LOG2E) * t)
            high = chain(base * grow, grow * grow)
            low = chain(base * shrink, shrink * shrink)
            vec, base, t = pair_base([row[:, LANES:] for row in rows], cols)
            for d in range(3):
                vectors[p, c, r, d * NA + at:d * NA + at + CHUNK, LANES:] = vec[d].astype(BF16)
            grow = jnp.exp2(side * t)
            both = chain(base * grow, grow * grow)
            tall.append([x.astype(BF16) for x in low[::-1] + high + both])
        wide = [jnp.concatenate([part[k] for part in tall], axis=0) for k in range(12)]
        return jnp.concatenate(wide, axis=1)

    def layer_one(p, c):
        gauss = jnp.concatenate([build(p, c, r) for r in range(group)], axis=0)
        scalar = jnp.dot(gauss, table_one[c], preferred_element_type=F32).astype(BF16)
        norms = []
        for r in range(group):
            vec = jnp.dot(vectors[p, c, r], table_vec[c], preferred_element_type=F32)
            one, two, three = [vec[d * NA:(d + 1) * NA] for d in range(3)]
            norms.append(((one * one + two * two + three * three) * scale_row).astype(BF16))
        norm = jnp.concatenate(norms, axis=0)
        update = jnp.dot(scalar, invariant[...], preferred_element_type=F32)
        update = update + jnp.dot(norm, magnitude[...], preferred_element_type=F32)
        own_rows = features[c * NA:(c + 1) * NA, :].astype(F32)
        half = 0.5 * update
        hidden = half * jnp.tanh(half) + half + jnp.concatenate([own_rows] * group, axis=0)
        second = jnp.dot(
            hidden.astype(BF16), later_projector[...], preferred_element_type=F32
        ).astype(BF16)
        out = lax.dot_general(w_two, second, NT, preferred_element_type=F32)
        flat = out[0:1] + out[1:2]
        rows = [flat[:, i * NA:(i + 1) * NA] for i in range(group)]
        return jnp.concatenate(rows, axis=0) + s_one[0:1, c * NA:(c + 1) * NA]

    def force(p, c, before, here, after):
        window = jnp.concatenate([before, here, after, jnp.zeros_like(after)], axis=1)
        high, low = split_bf16(window)
        stacked = jnp.concatenate([high.astype(F32), low.astype(F32)] * 2, axis=0).astype(BF16)
        result = jnp.zeros((group, 3 * NA), F32)
        for r in range(group):
            out = lax.dot_general(stacked, vectors[p, c, r], NT, preferred_element_type=F32)
            result = jnp.where(member_row == r, out[:group] + out[group:2 * group], result)
        return result

    order = [0] if cells == 1 else [0, cells - 1] + list(range(1, cells - 1))

    def is_moving(t):
        return jnp.where(t > 0, 1.0, 0.0).astype(F32)

    def s_copies(t, p):
        return [
            remote(s_send.at[t, p], s_recv.at[t, p, 1], s_send_sem.at[t, p, 0], s_recv_sem.at[t, p, 0], left),
            remote(s_send.at[t, p], s_recv.at[t, p, 0], s_send_sem.at[t, p, 1], s_recv_sem.at[t, p, 1], right),
        ]

    def vg_copies(t, p):
        return [
            remote(vg_send.at[t, p, 0], vg_recv.at[t, p, 1], vg_send_sem.at[t, p, 0], vg_recv_sem.at[t, p, 0], left),
            remote(vg_send.at[t, p, 1], vg_recv.at[t, p, 0], vg_send_sem.at[t, p, 1], vg_recv_sem.at[t, p, 1], right),
        ]

    def first_half(t, p):
        moving = is_moving(t)
        places_now = []
        for d in range(3):
            half = state_v[p, d] + (0.5 * step_time) * state_g[p, d]
            x = state_x[p, d] + (moving * step_time) * half
            state_v[p, d] = half
            state_x[p, d] = x
            if d == 2:
                x = x + shift
            places_now.append(x)
        for c in range(cells):
            for d in range(3):
                x = places_now[d]
                pieces = [x[:, at:at + NA] for at in (cell_at(c - 1), cell_at(c), cell_at(c + 1))]
                win[p, c, d, :, :] = jnp.concatenate(pieces + pieces[2:], axis=1)
        tall = jnp.concatenate(places_now + [jnp.zeros((-3 * group % 8, width), F32)], axis=0)
        for at in range(0, own, LANES):
            columns[p, at:at + LANES, :] = tall[:, at:at + LANES].T
        sources = {}
        sent = False
        for c in order:
            sources[c] = layer_one(p, c)
            if not sent and 0 in sources and cells - 1 in sources:
                sent = True
                s_send[t, p] = jnp.concatenate([sources[0], sources[cells - 1]], axis=1)
                for copy in s_copies(t, p):
                    copy.start()
        return sources

    def second_half(t, p, sources):
        moving = is_moving(t)
        forces = {}
        for c in order[2:]:
            forces[c] = force(p, c, sources[c - 1], sources[c], sources[c + 1])
        for copy in s_copies(t, p):
            copy.wait()
        sources[-1] = s_recv[t, p, 0, :, NA:2 * NA]
        sources[cells] = s_recv[t, p, 1, :, 0:NA]
        for c in order[:2]:
            forces[c] = force(p, c, sources[c - 1], sources[c], sources[c + 1])
        kinetic = jnp.zeros((group, 1), F32)
        for d in range(3):
            g = jnp.concatenate([forces[c][:, d * NA:(d + 1) * NA] for c in range(cells)], axis=1)
            v = state_v[p, d, :, 0:own] + (moving * (0.5 * step_time)) * g
            vg_send[t, p, 0, d] = jnp.concatenate([v[:, :NA], g[:, :NA]], axis=1)
            vg_send[t, p, 1, d] = jnp.concatenate([v[:, own - NA:], g[:, own - NA:]], axis=1)
            kinetic = kinetic + jnp.sum(v * v, axis=1, keepdims=True)
            state_v[p, d, :, 0:own] = v
            state_g[p, d, :, 0:own] = g
        across = jnp.sum(jnp.where(diagonal, kinetic, 0.0), axis=0, keepdims=True)
        kin_send[t, p] = across
        kin_recv[t, p, n - 1] = across

        def spread(d, inner):
            remote(
                kin_send.at[t, p], kin_recv.at[t, p, d - 1], kin_send_sem.at[t, p],
                kin_recv_sem.at[t, p], lax.rem(me + d, n),
            ).start()
            return inner

        lax.fori_loop(1, n, spread, 0)
        for copy in vg_copies(t, p):
            copy.start()

    def finish(t, p):
        everything = kin_recv.at[t, p, pl.ds(0, n - 1)]
        for copy in vg_copies(t, p):
            copy.wait()
        pltpu.make_async_copy(everything, everything, kin_send_sem.at[t, p]).wait()
        pltpu.make_async_copy(everything, everything, kin_recv_sem.at[t, p]).wait()
        collected = jnp.sum(kin_recv[t, p], axis=0)
        gathered = jnp.sum(jnp.where(diagonal, collected, 0.0), axis=1, keepdims=True)
        goal = target[p * group:(p + 1) * group]
        stretch = jnp.sqrt(goal / (gathered / (3.0 * own * n) + motion_work_lower_limit))
        stretch = jnp.where(t > 0, stretch, 1.0)
        rest = jnp.zeros((group, width - own - 2 * NA), F32)
        for d in range(3):
            from_left, from_right = vg_recv[t, p, 0, d], vg_recv[t, p, 1, d]
            state_v[p, d] = stretch * jnp.concatenate(
                [state_v[p, d, :, 0:own], from_right[:, :NA], from_left[:, :NA], rest], axis=1
            )
            state_g[p, d, :, right_at:right_at + NA] = from_right[:, NA:]
            state_g[p, d, :, left_at:left_at + NA] = from_left[:, NA:]

    def step(t, carry):
        sources = []
        for p in range(parts):
            pl.when(t > 0)(functools.partial(finish, t - 1, p))
            sources.append(first_half(t, p))
        for p in range(parts):
            second_half(t, p, sources[p])
        return carry

    lax.fori_loop(0, STEPS + 1, step, 0)
    for p in range(parts):
        finish(STEPS, p)

    def pick(values):
        result = jnp.zeros_like(values)
        for r in range(replicas):
            result = jnp.where(source == r, values[r:r + 1], result)
        return result

    def whole(state, d):
        return jnp.concatenate([state[p, d, :, 0:own] for p in range(parts)], axis=0)

    heat = jnp.sqrt(target / pick(target))
    floor = (
        me * cells + lax.broadcasted_iota(jnp.int32, (1, own), 1) // NA
    ).astype(F32)
    for d in range(3):
        x = pick(whole(state_x, d))
        if d == 2:
            x = x - floor
        places_out[d] = x
        speeds_out[d] = pick(whole(state_v, d)) * heat
        forces_out[d] = pick(whole(state_g, d))


def on_device(
    particle_places,
    particle_speeds,
    thermal_targets,
    element_features,
    swap_counterpart_slot,
    swap_approval_flags,
    initial_signal_projector,
    initial_distance_filter,
    initial_directional_scales,
    invariant_revision_matrix,
    magnitude_revision_matrix,
    later_signal_projector,
    later_directional_scales,
    push_output_matrix,
):
    n = lax.axis_size("dom")
    replicas, _, own = particle_places.shape
    cells = own // NA
    channels = element_features.shape[1]
    width = -(-(own + 2 * NA) // LANES) * LANES
    padded = -(-own // LANES) * LANES
    rounds = STEPS + 1
    parts = 2 if replicas % 2 == 0 else 1
    group = replicas // parts
    pad_rows = -(-3 * group // 8) * 8
    basis = initial_distance_filter.shape[0]
    depth = basis * 3 * NA
    vmem = pl.BlockSpec(memory_space=pltpu.VMEM)
    smem = pl.BlockSpec(memory_space=pltpu.SMEM)
    out = jax.ShapeDtypeStruct((3, replicas, own), F32)
    results = pl.pallas_call(
        functools.partial(kernel, n, replicas, cells, parts),
        out_shape=(out, out, out),
        in_specs=[vmem, vmem, smem, smem, smem] + [vmem] * 9,
        out_specs=(vmem, vmem, vmem),
        scratch_shapes=[
            pltpu.VMEM((2, NA, channels), BF16),
            pltpu.VMEM((3, replicas, LANES), F32),
            pltpu.VMEM((2, 3, replicas, LANES), F32),
            pltpu.VMEM((cells, depth, channels), BF16),
            pltpu.VMEM((cells, 4 * NA, channels), BF16),
            pltpu.VMEM((1, width), F32),
            pltpu.VMEM((parts, 3, group, width), F32),
            pltpu.VMEM((parts, 3, group, width), F32),
            pltpu.VMEM((parts, 3, group, width), F32),
            pltpu.VMEM((parts, cells, 3, group, 2 * LANES), F32),
            pltpu.VMEM((parts, padded, pad_rows), F32),
            pltpu.VMEM((parts, cells, group, 3 * NA, 2 * LANES), BF16),
            pltpu.VMEM((rounds, parts, group, LANES), F32),
            pltpu.VMEM((rounds, parts, 2, group, LANES), F32),
            pltpu.VMEM((rounds, parts, 2, 3, group, LANES), F32),
            pltpu.VMEM((rounds, parts, 2, 3, group, LANES), F32),
            pltpu.VMEM((rounds, parts, 1, LANES), F32),
            pltpu.VMEM((rounds, parts, n, 1, LANES), F32),
            pltpu.SemaphoreType.DMA((4,)),
            pltpu.SemaphoreType.DMA((4,)),
            pltpu.SemaphoreType.DMA((rounds, parts, 2)),
            pltpu.SemaphoreType.DMA((rounds, parts, 2)),
            pltpu.SemaphoreType.DMA((rounds, parts, 2)),
            pltpu.SemaphoreType.DMA((rounds, parts, 2)),
            pltpu.SemaphoreType.DMA((rounds, parts)),
            pltpu.SemaphoreType.DMA((rounds, parts)),
        ],
        compiler_params=pltpu.CompilerParams(
            collective_id=0, has_side_effects=True, vmem_limit_bytes=48 * 1024 * 1024
        ),
    )(
        jnp.transpose(particle_places, (1, 0, 2)),
        jnp.transpose(particle_speeds, (1, 0, 2)),
        thermal_targets,
        swap_counterpart_slot,
        swap_approval_flags,
        element_features,
        initial_signal_projector,
        initial_distance_filter,
        initial_directional_scales.reshape(1, -1),
        invariant_revision_matrix,
        magnitude_revision_matrix,
        later_signal_projector,
        later_directional_scales.reshape(1, -1),
        push_output_matrix.reshape(1, -1),
    )
    return tuple(jnp.transpose(result, (1, 0, 2)) for result in results)


def solution(mesh):
    along = P("groups", None, "dom")
    return jax.shard_map(
        on_device,
        mesh=mesh,
        in_specs=(
            along,
            along,
            P("groups"),
            P(("groups", "dom"), None),
            P("groups"),
            P("groups"),
            P(),
            P(),
            P(),
            P(),
            P(),
            P(),
            P(),
            P(),
        ),
        out_specs=(along, along, along),
        check_vma=False,
    )
```

```python
import functools
import math

import jax
import jax.numpy as jnp
from jax import lax
from jax.experimental import pallas as pl
from jax.experimental.pallas import tpu as pltpu
from jax.sharding import PartitionSpec as P

NA = 64
STEPS = 4
LANES = 128
CHUNK = 16
LOG2E = math.log2(math.e)

step_time = 0.05
motion_work_lower_limit = 1e-06

F32 = jnp.float32
BF16 = jnp.bfloat16
MESH = pl.DeviceIdType.MESH
NT = (((1,), (1,)), ((), ()))


def split_bf16(values):
    high = values.astype(BF16)
    low = (values - high.astype(F32)).astype(BF16)
    return high, low


def weight_rows(weights):
    high, low = split_bf16(weights)
    high, low = high.astype(F32), low.astype(F32)
    row = lax.broadcasted_iota(jnp.int32, (16, weights.shape[1]), 0)
    return jnp.where(row == 0, high, jnp.where(row == 1, low, 0.0)).astype(BF16)


def pair_base(rows, columns):
    dx, dy, dz = [row - column for row, column in zip(rows, columns)]
    squared = dx * dx + dy * dy + dz * dz
    inside = jnp.maximum(1.0 - squared, 0.0)
    envelope = inside * inside
    centered = 0.5 - inside
    base = jnp.exp2((centered * centered) * (-98.0 * LOG2E)) * envelope
    return (dx * envelope, dy * envelope, dz * envelope), base, centered


def kernel(
    n, inner, replicas, cells, parts,
    places, speeds, targets, slots, flags, features,
    projector, radial_filter, scales_one, invariant, magnitude, later_projector, scales_two, push,
    places_out, speeds_out, forces_out,
    feature_halo, place_send, place_halo, table_one, table_vec, s_one,
    state_x, state_v, state_g, win, columns, vectors,
    s_send, s_recv, vg_send, vg_recv, kin_send, kin_inner, kin_outer,
    init_send_sem, init_recv_sem, s_send_sem, s_recv_sem, vg_send_sem, vg_recv_sem,
    kin_send_sem, kin_recv_sem,
):
    me = lax.axis_index("dom")
    left = lax.rem(me + n - 1, n)
    right = lax.rem(me + 1, n)
    own = cells * NA
    width = state_x.shape[3]
    group = replicas // parts
    outer = n // inner
    right_at, left_at = own, own + NA
    channels = features.shape[1]

    def cell_at(c):
        return left_at if c < 0 else c * NA

    barrier = pltpu.get_barrier_semaphore()

    corner = me - lax.rem(me, inner)
    inner_peers = [corner + lax.rem(me + d, inner) for d in range(1, inner)]
    outer_peers = [lax.rem(me + d * inner, n) for d in range(1, outer)]
    greeted = [left, right] + inner_peers + outer_peers
    for peer in greeted:
        pl.semaphore_signal(barrier, inc=1, device_id={"dom": peer}, device_id_type=MESH)

    zeros_pad = jnp.zeros((group, width - own), F32)
    for d in range(3):
        x = places[d]
        place_send[d] = jnp.concatenate([x[:, :NA], x[:, own - NA:]], axis=1)
        for p in range(parts):
            members = slice(p * group, (p + 1) * group)
            state_x[p, d] = jnp.concatenate([x[members], zeros_pad], axis=1)
            state_v[p, d] = jnp.concatenate([speeds[d, members, :], zeros_pad], axis=1)
            state_g[p, d] = jnp.zeros((group, width), F32)

    pl.semaphore_wait(barrier, len(greeted))

    def remote(src, dst, send_sem, recv_sem, to):
        return pltpu.make_async_remote_copy(
            src_ref=src, dst_ref=dst, send_sem=send_sem, recv_sem=recv_sem,
            device_id={"dom": to}, device_id_type=MESH,
        )

    first = [
        remote(place_send, place_halo.at[1], init_send_sem.at[0], init_recv_sem.at[0], left),
        remote(place_send, place_halo.at[0], init_send_sem.at[1], init_recv_sem.at[1], right),
        remote(features.at[pl.ds(0, NA)], feature_halo.at[1], init_send_sem.at[2], init_recv_sem.at[2], left),
        remote(features.at[pl.ds(own - NA, NA)], feature_halo.at[0], init_send_sem.at[3], init_recv_sem.at[3], right),
    ]
    for copy in first:
        copy.start()

    basis = radial_filter.shape[0]
    offset = lax.broadcasted_iota(jnp.int32, radial_filter.shape, 0).astype(F32) - 0.5 * (basis - 1)
    filters = radial_filter[...] * jnp.exp(-2.0 * offset * offset)
    push_row = push[...]
    w_one = weight_rows(scales_one[...] * push_row)
    w_two = weight_rows(scales_two[...] * push_row)
    scale_row = scales_one[...] * scales_one[...]

    def make_table(rows):
        return jnp.dot(rows, projector[...], preferred_element_type=F32).astype(BF16)

    tables = {c: make_table(features[c * NA:(c + 1) * NA, :]) for c in range(cells)}
    for copy in first:
        copy.wait()
    tables[-1] = make_table(feature_halo[0])
    tables[cells] = make_table(feature_halo[1])

    s_parts = []
    for c in list(range(cells)) + [cells, -1]:
        out = lax.dot_general(w_one, tables[c], NT, preferred_element_type=F32)
        s_parts.append(out[0:1] + out[1:2])
    s_one[...] = jnp.concatenate(s_parts + [jnp.zeros((1, width - own - 2 * NA), F32)], axis=1)

    for c in range(cells):
        before, here, after = [tables[c + j].astype(F32) for j in (-1, 0, 1)]
        table_vec[c, 0:NA, :] = tables[c - 1]
        table_vec[c, NA:2 * NA, :] = tables[c]
        table_vec[c, 2 * NA:3 * NA, :] = tables[c + 1]
        table_vec[c, 3 * NA:4 * NA, :] = jnp.zeros((NA, channels), BF16)
        for k in range(8):
            row = filters[k:k + 1]
            table_one[c, k * LANES:k * LANES + NA, :] = (before * row).astype(BF16)
            table_one[c, k * LANES + NA:(k + 1) * LANES, :] = (here * row).astype(BF16)
        for j in range(4):
            at = (8 + j) * LANES
            table_one[c, at:at + NA, :] = (after * filters[4 + j:5 + j]).astype(BF16)
            table_one[c, at + NA:at + LANES, :] = (after * filters[3 - j:4 - j]).astype(BF16)

    for d in range(3):
        for p in range(parts):
            members = slice(p * group, (p + 1) * group)
            state_x[p, d, :, right_at:right_at + NA] = place_halo[1, d, members, 0:NA]
            state_x[p, d, :, left_at:left_at + NA] = place_halo[0, d, members, NA:2 * NA]

    total = float(cells * n)
    lane = lax.broadcasted_iota(jnp.int32, (1, width), 1)
    up = jnp.where(me == n - 1, total, 0.0).astype(F32)
    down = jnp.where(me == 0, -total, 0.0).astype(F32)
    shift = jnp.where(
        (lane >= right_at) & (lane < right_at + NA), up,
        jnp.where((lane >= left_at) & (lane < left_at + NA), down, 0.0),
    )
    side = jnp.where(lax.broadcasted_iota(jnp.int32, (1, LANES), 1) < NA, 14.0 * LOG2E, -14.0 * LOG2E).astype(F32)
    member_row = lax.broadcasted_iota(jnp.int32, (group, 1), 0)
    replica_row = lax.broadcasted_iota(jnp.int32, (replicas, 1), 0)
    diagonal = (
        lax.broadcasted_iota(jnp.int32, (group, LANES), 0)
        == lax.broadcasted_iota(jnp.int32, (group, LANES), 1)
    )
    target = jnp.zeros((replicas, 1), F32)
    source = jnp.zeros((replicas, 1), jnp.int32)
    for r in range(replicas):
        target = jnp.where(replica_row == r, targets[r], target)
        source = jnp.where(replica_row == r, jnp.where(flags[r] > 0, slots[r], r), source)

    def chain(start, power):
        values = [start]
        for _ in range(3):
            values.append(values[-1] * power)
        return values

    def build(p, c, r):
        rows = [win[p, c, d, r:r + 1, :] for d in range(3)]
        tall = []
        for at in range(0, NA, CHUNK):
            out = slice(at, at + CHUNK)
            cols = [
                columns[p, c * NA + at:c * NA + at + CHUNK, d * group + r:d * group + r + 1]
                for d in range(3)
            ]
            cols = [jnp.broadcast_to(col, (CHUNK, LANES)) for col in cols]
            vec, base, t = pair_base([row[:, :LANES] for row in rows], cols)
            for d in range(3):
                vectors[p, c, r, d * NA + at:d * NA + at + CHUNK, 0:LANES] = vec[d].astype(BF16)
            grow = jnp.exp2((14.0 * LOG2E) * t)
            shrink = jnp.exp2((-14.0 * LOG2E) * t)
            high = chain(base * grow, grow * grow)
            low = chain(base * shrink, shrink * shrink)
            vec, base, t = pair_base([row[:, LANES:] for row in rows], cols)
            for d in range(3):
                vectors[p, c, r, d * NA + at:d * NA + at + CHUNK, LANES:] = vec[d].astype(BF16)
            grow = jnp.exp2(side * t)
            both = chain(base * grow, grow * grow)
            tall.append([x.astype(BF16) for x in low[::-1] + high + both])
        wide = [jnp.concatenate([part[k] for part in tall], axis=0) for k in range(12)]
        return jnp.concatenate(wide, axis=1)

    def layer_one(p, c):
        gauss = jnp.concatenate([build(p, c, r) for r in range(group)], axis=0)
        scalar = jnp.dot(gauss, table_one[c], preferred_element_type=F32).astype(BF16)
        norms = []
        for r in range(group):
            vec = jnp.dot(vectors[p, c, r], table_vec[c], preferred_element_type=F32)
            one, two, three = [vec[d * NA:(d + 1) * NA] for d in range(3)]
            norms.append(((one * one + two * two + three * three) * scale_row).astype(BF16))
        norm = jnp.concatenate(norms, axis=0)
        update = jnp.dot(scalar, invariant[...], preferred_element_type=F32)
        update = update + jnp.dot(norm, magnitude[...], preferred_element_type=F32)
        own_rows = features[c * NA:(c + 1) * NA, :].astype(F32)
        half = 0.5 * update
        hidden = half * jnp.tanh(half) + half + jnp.concatenate([own_rows] * group, axis=0)
        second = jnp.dot(
            hidden.astype(BF16), later_projector[...], preferred_element_type=F32
        ).astype(BF16)
        out = lax.dot_general(w_two, second, NT, preferred_element_type=F32)
        flat = out[0:1] + out[1:2]
        rows = [flat[:, i * NA:(i + 1) * NA] for i in range(group)]
        return jnp.concatenate(rows, axis=0) + s_one[0:1, c * NA:(c + 1) * NA]

    def force(p, c, before, here, after):
        window = jnp.concatenate([before, here, after, jnp.zeros_like(after)], axis=1)
        high, low = split_bf16(window)
        stacked = jnp.concatenate([high.astype(F32), low.astype(F32)] * 2, axis=0).astype(BF16)
        result = jnp.zeros((group, 3 * NA), F32)
        for r in range(group):
            out = lax.dot_general(stacked, vectors[p, c, r], NT, preferred_element_type=F32)
            result = jnp.where(member_row == r, out[:group] + out[group:2 * group], result)
        return result

    order = [0] if cells == 1 else [0, cells - 1] + list(range(1, cells - 1))

    def is_moving(t):
        return jnp.where(t > 0, 1.0, 0.0).astype(F32)

    def s_copies(t, p):
        return [
            remote(s_send.at[t, p], s_recv.at[t, p, 1], s_send_sem.at[t, p, 0], s_recv_sem.at[t, p, 0], left),
            remote(s_send.at[t, p], s_recv.at[t, p, 0], s_send_sem.at[t, p, 1], s_recv_sem.at[t, p, 1], right),
        ]

    def vg_copies(t, p):
        return [
            remote(vg_send.at[t, p, 0], vg_recv.at[t, p, 1], vg_send_sem.at[t, p, 0], vg_recv_sem.at[t, p, 0], left),
            remote(vg_send.at[t, p, 1], vg_recv.at[t, p, 0], vg_send_sem.at[t, p, 1], vg_recv_sem.at[t, p, 1], right),
        ]

    def first_half(t, p, between):
        moving = is_moving(t)
        places_now = []
        for d in range(3):
            half = state_v[p, d] + (0.5 * step_time) * state_g[p, d]
            x = state_x[p, d] + (moving * step_time) * half
            state_v[p, d] = half
            state_x[p, d] = x
            if d == 2:
                x = x + shift
            places_now.append(x)
        for c in range(cells):
            for d in range(3):
                x = places_now[d]
                pieces = [x[:, at:at + NA] for at in (cell_at(c - 1), cell_at(c), cell_at(c + 1))]
                win[p, c, d, :, :] = jnp.concatenate(pieces + pieces[2:], axis=1)
        tall = jnp.concatenate(places_now + [jnp.zeros((-3 * group % 8, width), F32)], axis=0)
        for at in range(0, own, LANES):
            columns[p, at:at + LANES, :] = tall[:, at:at + LANES].T
        sources = {}
        sent = False
        for c in order:
            sources[c] = layer_one(p, c)
            if not sent and 0 in sources and cells - 1 in sources:
                sent = True
                s_send[t, p] = jnp.concatenate([sources[0], sources[cells - 1]], axis=1)
                for copy in s_copies(t, p):
                    copy.start()
                between()
        return sources

    def second_half(t, p, sources):
        moving = is_moving(t)
        forces = {}
        for c in order[2:]:
            forces[c] = force(p, c, sources[c - 1], sources[c], sources[c + 1])
        for copy in s_copies(t, p):
            copy.wait()
        sources[-1] = s_recv[t, p, 0, :, NA:2 * NA]
        sources[cells] = s_recv[t, p, 1, :, 0:NA]
        for c in order[:2]:
            forces[c] = force(p, c, sources[c - 1], sources[c], sources[c + 1])
        kinetic = jnp.zeros((group, 1), F32)
        for d in range(3):
            g = jnp.concatenate([forces[c][:, d * NA:(d + 1) * NA] for c in range(cells)], axis=1)
            v = state_v[p, d, :, 0:own] + (moving * (0.5 * step_time)) * g
            vg_send[t, p, 0, d] = jnp.concatenate([v[:, :NA], g[:, :NA]], axis=1)
            vg_send[t, p, 1, d] = jnp.concatenate([v[:, own - NA:], g[:, own - NA:]], axis=1)
            kinetic = kinetic + jnp.sum(v * v, axis=1, keepdims=True)
            state_v[p, d, :, 0:own] = v
            state_g[p, d, :, 0:own] = g
        across = jnp.sum(jnp.where(diagonal, kinetic, 0.0), axis=0, keepdims=True)
        kin_send[t, p, 0] = across
        kin_inner[t, p, inner - 1] = across
        for slot, peer in enumerate(inner_peers):
            remote(
                kin_send.at[t, p, 0], kin_inner.at[t, p, slot], kin_send_sem.at[t, p, 0],
                kin_recv_sem.at[t, p, 0], peer,
            ).start()
        for copy in vg_copies(t, p):
            copy.start()

    def wait_all(buffer, count, t, p, stage):
        if count > 0:
            everything = buffer.at[t, p, pl.ds(0, count)]
            pltpu.make_async_copy(everything, everything, kin_send_sem.at[t, p, stage]).wait()
            pltpu.make_async_copy(everything, everything, kin_recv_sem.at[t, p, stage]).wait()

    def relay(t, p):
        wait_all(kin_inner, inner - 1, t, p, 0)
        partial = jnp.sum(kin_inner[t, p], axis=0)
        kin_send[t, p, 1] = partial
        kin_outer[t, p, outer - 1] = partial
        for slot, peer in enumerate(outer_peers):
            remote(
                kin_send.at[t, p, 1], kin_outer.at[t, p, slot], kin_send_sem.at[t, p, 1],
                kin_recv_sem.at[t, p, 1], peer,
            ).start()

    def finish(t, p):
        for copy in vg_copies(t, p):
            copy.wait()
        wait_all(kin_outer, outer - 1, t, p, 1)
        collected = jnp.sum(kin_outer[t, p], axis=0)
        gathered = jnp.sum(jnp.where(diagonal, collected, 0.0), axis=1, keepdims=True)
        goal = target[p * group:(p + 1) * group]
        stretch = jnp.sqrt(goal / (gathered / (3.0 * own * n) + motion_work_lower_limit))
        stretch = jnp.where(t > 0, stretch, 1.0)
        rest = jnp.zeros((group, width - own - 2 * NA), F32)
        for d in range(3):
            from_left, from_right = vg_recv[t, p, 0, d], vg_recv[t, p, 1, d]
            state_v[p, d] = stretch * jnp.concatenate(
                [state_v[p, d, :, 0:own], from_right[:, :NA], from_left[:, :NA], rest], axis=1
            )
            state_g[p, d, :, right_at:right_at + NA] = from_right[:, NA:]
            state_g[p, d, :, left_at:left_at + NA] = from_left[:, NA:]

    def later(t, action, p):
        pl.when(t > 0)(functools.partial(action, t - 1, p))

    def step(t, carry):
        later(t, finish, 0)
        sources = first_half(t, 0, lambda: later(t, relay, 1))
        later(t, finish, 1)
        others = first_half(t, 1, lambda: second_half(t, 0, sources))
        relay(t, 0)
        second_half(t, 1, others)
        return carry

    lax.fori_loop(0, STEPS + 1, step, 0)
    relay(STEPS, 1)
    for p in range(parts):
        finish(STEPS, p)

    def pick(values):
        result = jnp.zeros_like(values)
        for r in range(replicas):
            result = jnp.where(source == r, values[r:r + 1], result)
        return result

    def whole(state, d):
        return jnp.concatenate([state[p, d, :, 0:own] for p in range(parts)], axis=0)

    heat = jnp.sqrt(target / pick(target))
    floor = (
        me * cells + lax.broadcasted_iota(jnp.int32, (1, own), 1) // NA
    ).astype(F32)
    for d in range(3):
        x = pick(whole(state_x, d))
        if d == 2:
            x = x - floor
        places_out[d] = x
        speeds_out[d] = pick(whole(state_v, d)) * heat
        forces_out[d] = pick(whole(state_g, d))


def on_device(
    particle_places,
    particle_speeds,
    thermal_targets,
    element_features,
    swap_counterpart_slot,
    swap_approval_flags,
    initial_signal_projector,
    initial_distance_filter,
    initial_directional_scales,
    invariant_revision_matrix,
    magnitude_revision_matrix,
    later_signal_projector,
    later_directional_scales,
    push_output_matrix,
):
    n = lax.axis_size("dom")
    replicas, _, own = particle_places.shape
    cells = own // NA
    channels = element_features.shape[1]
    width = -(-(own + 2 * NA) // LANES) * LANES
    padded = -(-own // LANES) * LANES
    rounds = STEPS + 1
    parts = 2
    inner = max(d for d in range(1, n + 1) if n % d == 0 and d * d <= n)
    group = replicas // parts
    pad_rows = -(-3 * group // 8) * 8
    basis = initial_distance_filter.shape[0]
    depth = basis * 3 * NA
    vmem = pl.BlockSpec(memory_space=pltpu.VMEM)
    smem = pl.BlockSpec(memory_space=pltpu.SMEM)
    out = jax.ShapeDtypeStruct((3, replicas, own), F32)
    results = pl.pallas_call(
        functools.partial(kernel, n, inner, replicas, cells, parts),
        out_shape=(out, out, out),
        in_specs=[vmem, vmem, smem, smem, smem] + [vmem] * 9,
        out_specs=(vmem, vmem, vmem),
        scratch_shapes=[
            pltpu.VMEM((2, NA, channels), BF16),
            pltpu.VMEM((3, replicas, LANES), F32),
            pltpu.VMEM((2, 3, replicas, LANES), F32),
            pltpu.VMEM((cells, depth, channels), BF16),
            pltpu.VMEM((cells, 4 * NA, channels), BF16),
            pltpu.VMEM((1, width), F32),
            pltpu.VMEM((parts, 3, group, width), F32),
            pltpu.VMEM((parts, 3, group, width), F32),
            pltpu.VMEM((parts, 3, group, width), F32),
            pltpu.VMEM((parts, cells, 3, group, 2 * LANES), F32),
            pltpu.VMEM((parts, padded, pad_rows), F32),
            pltpu.VMEM((parts, cells, group, 3 * NA, 2 * LANES), BF16),
            pltpu.VMEM((rounds, parts, group, LANES), F32),
            pltpu.VMEM((rounds, parts, 2, group, LANES), F32),
            pltpu.VMEM((rounds, parts, 2, 3, group, LANES), F32),
            pltpu.VMEM((rounds, parts, 2, 3, group, LANES), F32),
            pltpu.VMEM((rounds, parts, 2, 1, LANES), F32),
            pltpu.VMEM((rounds, parts, inner, 1, LANES), F32),
            pltpu.VMEM((rounds, parts, n // inner, 1, LANES), F32),
            pltpu.SemaphoreType.DMA((4,)),
            pltpu.SemaphoreType.DMA((4,)),
            pltpu.SemaphoreType.DMA((rounds, parts, 2)),
            pltpu.SemaphoreType.DMA((rounds, parts, 2)),
            pltpu.SemaphoreType.DMA((rounds, parts, 2)),
            pltpu.SemaphoreType.DMA((rounds, parts, 2)),
            pltpu.SemaphoreType.DMA((rounds, parts, 2)),
            pltpu.SemaphoreType.DMA((rounds, parts, 2)),
        ],
        compiler_params=pltpu.CompilerParams(
            collective_id=0, has_side_effects=True, vmem_limit_bytes=48 * 1024 * 1024
        ),
    )(
        jnp.transpose(particle_places, (1, 0, 2)),
        jnp.transpose(particle_speeds, (1, 0, 2)),
        thermal_targets,
        swap_counterpart_slot,
        swap_approval_flags,
        element_features,
        initial_signal_projector,
        initial_distance_filter,
        initial_directional_scales.reshape(1, -1),
        invariant_revision_matrix,
        magnitude_revision_matrix,
        later_signal_projector,
        later_directional_scales.reshape(1, -1),
        push_output_matrix.reshape(1, -1),
    )
    return tuple(jnp.transpose(result, (1, 0, 2)) for result in results)


def solution(mesh):
    along = P("groups", None, "dom")
    return jax.shard_map(
        on_device,
        mesh=mesh,
        in_specs=(
            along,
            along,
            P("groups"),
            P(("groups", "dom"), None),
            P("groups"),
            P("groups"),
            P(),
            P(),
            P(),
            P(),
            P(),
            P(),
            P(),
            P(),
        ),
        out_specs=(along, along, along),
        check_vma=False,
    )
```

```python
import functools
import math

import jax
import jax.numpy as jnp
from jax import lax
from jax.experimental import pallas as pl
from jax.experimental.pallas import tpu as pltpu
from jax.sharding import PartitionSpec as P

NA = 64
STEPS = 4
LANES = 128
CHUNK = 16
LOG2E = math.log2(math.e)

step_time = 0.05
motion_work_lower_limit = 1e-06

F32 = jnp.float32
BF16 = jnp.bfloat16
MESH = pl.DeviceIdType.MESH
NT = (((1,), (1,)), ((), ()))


def split_bf16(values):
    high = values.astype(BF16)
    low = (values - high.astype(F32)).astype(BF16)
    return high, low


def weight_rows(weights):
    high, low = split_bf16(weights)
    high, low = high.astype(F32), low.astype(F32)
    row = lax.broadcasted_iota(jnp.int32, (16, weights.shape[1]), 0)
    return jnp.where(row == 0, high, jnp.where(row == 1, low, 0.0)).astype(BF16)


def pair_base(rows, columns):
    dx, dy, dz = [row - column for row, column in zip(rows, columns)]
    squared = dx * dx + dy * dy + dz * dz
    inside = jnp.maximum(1.0 - squared, 0.0)
    envelope = inside * inside
    centered = 0.5 - inside
    base = jnp.exp2((centered * centered) * (-98.0 * LOG2E)) * envelope
    return (dx * envelope, dy * envelope, dz * envelope), base, centered


def kernel(
    n, replicas, cells, parts,
    places, speeds, targets, slots, flags, features,
    projector, radial_filter, scales_one, invariant, magnitude, later_projector, scales_two, push,
    places_out, speeds_out, forces_out,
    feature_halo, place_send, place_halo, table_one, table_vec, s_one,
    state_x, state_v, state_g, win, columns, vectors,
    s_send, s_recv, vg_send, vg_recv, kin_send, kin_recv,
    init_send_sem, init_recv_sem, s_send_sem, s_recv_sem, vg_send_sem, vg_recv_sem,
    kin_send_sem, kin_recv_sem,
):
    me = lax.axis_index("dom")
    left = lax.rem(me + n - 1, n)
    right = lax.rem(me + 1, n)
    own = cells * NA
    width = state_x.shape[3]
    group = replicas // parts
    right_at, left_at = own, own + NA
    channels = features.shape[1]

    def cell_at(c):
        return left_at if c < 0 else c * NA

    barrier = pltpu.get_barrier_semaphore()

    def greet(d, carry):
        pl.semaphore_signal(barrier, inc=1, device_id={"dom": lax.rem(me + d, n)}, device_id_type=MESH)
        return carry

    lax.fori_loop(1, n, greet, 0)

    zeros_pad = jnp.zeros((group, width - own), F32)
    for d in range(3):
        x = places[d]
        place_send[d] = jnp.concatenate([x[:, :NA], x[:, own - NA:]], axis=1)
        for p in range(parts):
            members = slice(p * group, (p + 1) * group)
            state_x[p, d] = jnp.concatenate([x[members], zeros_pad], axis=1)
            state_v[p, d] = jnp.concatenate([speeds[d, members, :], zeros_pad], axis=1)
            state_g[p, d] = jnp.zeros((group, width), F32)

    pl.semaphore_wait(barrier, n - 1)

    def remote(src, dst, send_sem, recv_sem, to):
        return pltpu.make_async_remote_copy(
            src_ref=src, dst_ref=dst, send_sem=send_sem, recv_sem=recv_sem,
            device_id={"dom": to}, device_id_type=MESH,
        )

    first = [
        remote(place_send, place_halo.at[1], init_send_sem.at[0], init_recv_sem.at[0], left),
        remote(place_send, place_halo.at[0], init_send_sem.at[1], init_recv_sem.at[1], right),
        remote(features.at[pl.ds(0, NA)], feature_halo.at[1], init_send_sem.at[2], init_recv_sem.at[2], left),
        remote(features.at[pl.ds(own - NA, NA)], feature_halo.at[0], init_send_sem.at[3], init_recv_sem.at[3], right),
    ]
    for copy in first:
        copy.start()

    basis = radial_filter.shape[0]
    offset = lax.broadcasted_iota(jnp.int32, radial_filter.shape, 0).astype(F32) - 0.5 * (basis - 1)
    filters = radial_filter[...] * jnp.exp(-2.0 * offset * offset)
    push_row = push[...]
    w_one = weight_rows(scales_one[...] * push_row)
    w_two = weight_rows(scales_two[...] * push_row)
    scale_row = scales_one[...] * scales_one[...]

    def make_table(rows):
        return jnp.dot(rows, projector[...], preferred_element_type=F32).astype(BF16)

    tables = {c: make_table(features[c * NA:(c + 1) * NA, :]) for c in range(cells)}
    for copy in first:
        copy.wait()
    tables[-1] = make_table(feature_halo[0])
    tables[cells] = make_table(feature_halo[1])

    s_parts = []
    for c in list(range(cells)) + [cells, -1]:
        out = lax.dot_general(w_one, tables[c], NT, preferred_element_type=F32)
        s_parts.append(out[0:1] + out[1:2])
    s_one[...] = jnp.concatenate(s_parts + [jnp.zeros((1, width - own - 2 * NA), F32)], axis=1)

    for c in range(cells):
        before, here, after = [tables[c + j].astype(F32) for j in (-1, 0, 1)]
        table_vec[c, 0:NA, :] = tables[c - 1]
        table_vec[c, NA:2 * NA, :] = tables[c]
        table_vec[c, 2 * NA:3 * NA, :] = tables[c + 1]
        table_vec[c, 3 * NA:4 * NA, :] = jnp.zeros((NA, channels), BF16)
        for k in range(8):
            row = filters[k:k + 1]
            table_one[c, k * LANES:k * LANES + NA, :] = (before * row).astype(BF16)
            table_one[c, k * LANES + NA:(k + 1) * LANES, :] = (here * row).astype(BF16)
        for j in range(4):
            at = (8 + j) * LANES
            table_one[c, at:at + NA, :] = (after * filters[4 + j:5 + j]).astype(BF16)
            table_one[c, at + NA:at + LANES, :] = (after * filters[3 - j:4 - j]).astype(BF16)

    for d in range(3):
        for p in range(parts):
            members = slice(p * group, (p + 1) * group)
            state_x[p, d, :, right_at:right_at + NA] = place_halo[1, d, members, 0:NA]
            state_x[p, d, :, left_at:left_at + NA] = place_halo[0, d, members, NA:2 * NA]

    total = float(cells * n)
    lane = lax.broadcasted_iota(jnp.int32, (1, width), 1)
    up = jnp.where(me == n - 1, total, 0.0).astype(F32)
    down = jnp.where(me == 0, -total, 0.0).astype(F32)
    shift = jnp.where(
        (lane >= right_at) & (lane < right_at + NA), up,
        jnp.where((lane >= left_at) & (lane < left_at + NA), down, 0.0),
    )
    side = jnp.where(lax.broadcasted_iota(jnp.int32, (1, LANES), 1) < NA, 14.0 * LOG2E, -14.0 * LOG2E).astype(F32)
    member_row = lax.broadcasted_iota(jnp.int32, (group, 1), 0)
    replica_row = lax.broadcasted_iota(jnp.int32, (replicas, 1), 0)
    diagonals = [
        lax.broadcasted_iota(jnp.int32, (group, LANES), 0) + p * group
        == lax.broadcasted_iota(jnp.int32, (group, LANES), 1)
        for p in range(parts)
    ]
    target = jnp.zeros((replicas, 1), F32)
    source = jnp.zeros((replicas, 1), jnp.int32)
    for r in range(replicas):
        target = jnp.where(replica_row == r, targets[r], target)
        source = jnp.where(replica_row == r, jnp.where(flags[r] > 0, slots[r], r), source)

    def chain(start, power):
        values = [start]
        for _ in range(3):
            values.append(values[-1] * power)
        return values

    def build(p, c, r):
        rows = [win[p, c, d, r:r + 1, :] for d in range(3)]
        tall = []
        for at in range(0, NA, CHUNK):
            out = slice(at, at + CHUNK)
            cols = [
                columns[p, c * NA + at:c * NA + at + CHUNK, d * group + r:d * group + r + 1]
                for d in range(3)
            ]
            cols = [jnp.broadcast_to(col, (CHUNK, LANES)) for col in cols]
            vec, base, t = pair_base([row[:, :LANES] for row in rows], cols)
            for d in range(3):
                vectors[p, c, r, d * NA + at:d * NA + at + CHUNK, 0:LANES] = vec[d].astype(BF16)
            grow = jnp.exp2((14.0 * LOG2E) * t)
            shrink = jnp.exp2((-14.0 * LOG2E) * t)
            high = chain(base * grow, grow * grow)
            low = chain(base * shrink, shrink * shrink)
            vec, base, t = pair_base([row[:, LANES:] for row in rows], cols)
            for d in range(3):
                vectors[p, c, r, d * NA + at:d * NA + at + CHUNK, LANES:] = vec[d].astype(BF16)
            grow = jnp.exp2(side * t)
            both = chain(base * grow, grow * grow)
            tall.append([x.astype(BF16) for x in low[::-1] + high + both])
        wide = [jnp.concatenate([part[k] for part in tall], axis=0) for k in range(12)]
        return jnp.concatenate(wide, axis=1)

    def layer_one(p, c):
        gauss = jnp.concatenate([build(p, c, r) for r in range(group)], axis=0)
        scalar = jnp.dot(gauss, table_one[c], preferred_element_type=F32).astype(BF16)
        norms = []
        for r in range(group):
            vec = jnp.dot(vectors[p, c, r], table_vec[c], preferred_element_type=F32)
            one, two, three = [vec[d * NA:(d + 1) * NA] for d in range(3)]
            norms.append(((one * one + two * two + three * three) * scale_row).astype(BF16))
        norm = jnp.concatenate(norms, axis=0)
        update = jnp.dot(scalar, invariant[...], preferred_element_type=F32)
        update = update + jnp.dot(norm, magnitude[...], preferred_element_type=F32)
        own_rows = features[c * NA:(c + 1) * NA, :].astype(F32)
        half = 0.5 * update
        hidden = half * jnp.tanh(half) + half + jnp.concatenate([own_rows] * group, axis=0)
        second = jnp.dot(
            hidden.astype(BF16), later_projector[...], preferred_element_type=F32
        ).astype(BF16)
        out = lax.dot_general(w_two, second, NT, preferred_element_type=F32)
        flat = out[0:1] + out[1:2]
        rows = [flat[:, i * NA:(i + 1) * NA] for i in range(group)]
        return jnp.concatenate(rows, axis=0) + s_one[0:1, c * NA:(c + 1) * NA]

    def force(p, c, before, here, after):
        window = jnp.concatenate([before, here, after, jnp.zeros_like(after)], axis=1)
        high, low = split_bf16(window)
        stacked = jnp.concatenate([high.astype(F32), low.astype(F32)] * 2, axis=0).astype(BF16)
        result = jnp.zeros((group, 3 * NA), F32)
        for r in range(group):
            out = lax.dot_general(stacked, vectors[p, c, r], NT, preferred_element_type=F32)
            result = jnp.where(member_row == r, out[:group] + out[group:2 * group], result)
        return result

    order = [0] if cells == 1 else [0, cells - 1] + list(range(1, cells - 1))

    def is_moving(t):
        return jnp.where(t > 0, 1.0, 0.0).astype(F32)

    def s_copies(t, p):
        return [
            remote(s_send.at[t, p], s_recv.at[t, p, 1], s_send_sem.at[t, p, 0], s_recv_sem.at[t, p, 0], left),
            remote(s_send.at[t, p], s_recv.at[t, p, 0], s_send_sem.at[t, p, 1], s_recv_sem.at[t, p, 1], right),
        ]

    def vg_copies(t, p):
        return [
            remote(vg_send.at[t, p, 0], vg_recv.at[t, p, 1], vg_send_sem.at[t, p, 0], vg_recv_sem.at[t, p, 0], left),
            remote(vg_send.at[t, p, 1], vg_recv.at[t, p, 0], vg_send_sem.at[t, p, 1], vg_recv_sem.at[t, p, 1], right),
        ]

    def first_half(t, p):
        moving = is_moving(t)
        places_now = []
        for d in range(3):
            half = state_v[p, d] + (0.5 * step_time) * state_g[p, d]
            x = state_x[p, d] + (moving * step_time) * half
            state_v[p, d] = half
            state_x[p, d] = x
            if d == 2:
                x = x + shift
            places_now.append(x)
        for c in range(cells):
            for d in range(3):
                x = places_now[d]
                pieces = [x[:, at:at + NA] for at in (cell_at(c - 1), cell_at(c), cell_at(c + 1))]
                win[p, c, d, :, :] = jnp.concatenate(pieces + pieces[2:], axis=1)
        tall = jnp.concatenate(places_now + [jnp.zeros((-3 * group % 8, width), F32)], axis=0)
        for at in range(0, own, LANES):
            columns[p, at:at + LANES, :] = tall[:, at:at + LANES].T
        sources = {}
        sent = False
        for c in order:
            sources[c] = layer_one(p, c)
            if not sent and 0 in sources and cells - 1 in sources:
                sent = True
                s_send[t, p] = jnp.concatenate([sources[0], sources[cells - 1]], axis=1)
                for copy in s_copies(t, p):
                    copy.start()
        return sources

    def second_half(t, p, sources):
        moving = is_moving(t)
        forces = {}
        for c in order[2:]:
            forces[c] = force(p, c, sources[c - 1], sources[c], sources[c + 1])
        for copy in s_copies(t, p):
            copy.wait_recv()
        sources[-1] = s_recv[t, p, 0, :, NA:2 * NA]
        sources[cells] = s_recv[t, p, 1, :, 0:NA]
        for c in order[:2]:
            forces[c] = force(p, c, sources[c - 1], sources[c], sources[c + 1])
        kinetic = jnp.zeros((group, 1), F32)
        for d in range(3):
            g = jnp.concatenate([forces[c][:, d * NA:(d + 1) * NA] for c in range(cells)], axis=1)
            v = state_v[p, d, :, 0:own] + (moving * (0.5 * step_time)) * g
            vg_send[t, p, 0, d] = jnp.concatenate([v[:, :NA], g[:, :NA]], axis=1)
            vg_send[t, p, 1, d] = jnp.concatenate([v[:, own - NA:], g[:, own - NA:]], axis=1)
            kinetic = kinetic + jnp.sum(v * v, axis=1, keepdims=True)
            state_v[p, d, :, 0:own] = v
            state_g[p, d, :, 0:own] = g
        for copy in vg_copies(t, p):
            copy.start()
        return jnp.sum(jnp.where(diagonals[p], kinetic, 0.0), axis=0, keepdims=True)

    def spread_kinetic(t, across):
        kin_send[t] = across
        kin_recv[t, n - 1] = across

        def spread(d, inner):
            remote(
                kin_send.at[t], kin_recv.at[t, d - 1], kin_send_sem.at[t], kin_recv_sem.at[t],
                lax.rem(me + d, n),
            ).start()
            return inner

        lax.fori_loop(1, n, spread, 0)

    def wait_kinetic(t, sem):
        everything = kin_recv.at[t, pl.ds(0, n - 1)]
        pltpu.make_async_copy(everything, everything, sem.at[t]).wait()

    def finish(t, p):
        if p == 0:
            wait_kinetic(t, kin_recv_sem)
        for copy in vg_copies(t, p):
            copy.wait_recv()
        collected = jnp.sum(kin_recv[t], axis=0)
        gathered = jnp.sum(jnp.where(diagonals[p], collected, 0.0), axis=1, keepdims=True)
        goal = target[p * group:(p + 1) * group]
        stretch = jnp.sqrt(goal / (gathered / (3.0 * own * n) + motion_work_lower_limit))
        stretch = jnp.where(t > 0, stretch, 1.0)
        rest = jnp.zeros((group, width - own - 2 * NA), F32)
        for d in range(3):
            from_left, from_right = vg_recv[t, p, 0, d], vg_recv[t, p, 1, d]
            state_v[p, d] = stretch * jnp.concatenate(
                [state_v[p, d, :, 0:own], from_right[:, :NA], from_left[:, :NA], rest], axis=1
            )
            state_g[p, d, :, right_at:right_at + NA] = from_right[:, NA:]
            state_g[p, d, :, left_at:left_at + NA] = from_left[:, NA:]

    def step(t, carry):
        sources = []
        for p in range(parts):
            pl.when(t > 0)(functools.partial(finish, t - 1, p))
            sources.append(first_half(t, p))
        spread_kinetic(t, sum(second_half(t, p, sources[p]) for p in range(parts)))
        return carry

    lax.fori_loop(0, STEPS + 1, step, 0)
    for p in range(parts):
        finish(STEPS, p)

    def drain(t, carry):
        wait_kinetic(t, kin_send_sem)
        for p in range(parts):
            for copy in s_copies(t, p) + vg_copies(t, p):
                copy.wait_send()
        return carry

    lax.fori_loop(0, STEPS + 1, drain, 0)

    def pick(values):
        result = jnp.zeros_like(values)
        for r in range(replicas):
            result = jnp.where(source == r, values[r:r + 1], result)
        return result

    def whole(state, d):
        return jnp.concatenate([state[p, d, :, 0:own] for p in range(parts)], axis=0)

    heat = jnp.sqrt(target / pick(target))
    floor = (
        me * cells + lax.broadcasted_iota(jnp.int32, (1, own), 1) // NA
    ).astype(F32)
    for d in range(3):
        x = pick(whole(state_x, d))
        if d == 2:
            x = x - floor
        places_out[d] = x
        speeds_out[d] = pick(whole(state_v, d)) * heat
        forces_out[d] = pick(whole(state_g, d))


def on_device(
    particle_places,
    particle_speeds,
    thermal_targets,
    element_features,
    swap_counterpart_slot,
    swap_approval_flags,
    initial_signal_projector,
    initial_distance_filter,
    initial_directional_scales,
    invariant_revision_matrix,
    magnitude_revision_matrix,
    later_signal_projector,
    later_directional_scales,
    push_output_matrix,
):
    n = lax.axis_size("dom")
    replicas, _, own = particle_places.shape
    cells = own // NA
    channels = element_features.shape[1]
    width = -(-(own + 2 * NA) // LANES) * LANES
    padded = -(-own // LANES) * LANES
    rounds = STEPS + 1
    parts = 2 if replicas % 2 == 0 else 1
    group = replicas // parts
    pad_rows = -(-3 * group // 8) * 8
    basis = initial_distance_filter.shape[0]
    depth = basis * 3 * NA
    vmem = pl.BlockSpec(memory_space=pltpu.VMEM)
    smem = pl.BlockSpec(memory_space=pltpu.SMEM)
    out = jax.ShapeDtypeStruct((3, replicas, own), F32)
    results = pl.pallas_call(
        functools.partial(kernel, n, replicas, cells, parts),
        out_shape=(out, out, out),
        in_specs=[vmem, vmem, smem, smem, smem] + [vmem] * 9,
        out_specs=(vmem, vmem, vmem),
        scratch_shapes=[
            pltpu.VMEM((2, NA, channels), BF16),
            pltpu.VMEM((3, replicas, LANES), F32),
            pltpu.VMEM((2, 3, replicas, LANES), F32),
            pltpu.VMEM((cells, depth, channels), BF16),
            pltpu.VMEM((cells, 4 * NA, channels), BF16),
            pltpu.VMEM((1, width), F32),
            pltpu.VMEM((parts, 3, group, width), F32),
            pltpu.VMEM((parts, 3, group, width), F32),
            pltpu.VMEM((parts, 3, group, width), F32),
            pltpu.VMEM((parts, cells, 3, group, 2 * LANES), F32),
            pltpu.VMEM((parts, padded, pad_rows), F32),
            pltpu.VMEM((parts, cells, group, 3 * NA, 2 * LANES), BF16),
            pltpu.VMEM((rounds, parts, group, LANES), F32),
            pltpu.VMEM((rounds, parts, 2, group, LANES), F32),
            pltpu.VMEM((rounds, parts, 2, 3, group, LANES), F32),
            pltpu.VMEM((rounds, parts, 2, 3, group, LANES), F32),
            pltpu.VMEM((rounds, 1, LANES), F32),
            pltpu.VMEM((rounds, n, 1, LANES), F32),
            pltpu.SemaphoreType.DMA((4,)),
            pltpu.SemaphoreType.DMA((4,)),
            pltpu.SemaphoreType.DMA((rounds, parts, 2)),
            pltpu.SemaphoreType.DMA((rounds, parts, 2)),
            pltpu.SemaphoreType.DMA((rounds, parts, 2)),
            pltpu.SemaphoreType.DMA((rounds, parts, 2)),
            pltpu.SemaphoreType.DMA((rounds,)),
            pltpu.SemaphoreType.DMA((rounds,)),
        ],
        compiler_params=pltpu.CompilerParams(
            collective_id=0, has_side_effects=True, vmem_limit_bytes=48 * 1024 * 1024
        ),
    )(
        jnp.transpose(particle_places, (1, 0, 2)),
        jnp.transpose(particle_speeds, (1, 0, 2)),
        thermal_targets,
        swap_counterpart_slot,
        swap_approval_flags,
        element_features,
        initial_signal_projector,
        initial_distance_filter,
        initial_directional_scales.reshape(1, -1),
        invariant_revision_matrix,
        magnitude_revision_matrix,
        later_signal_projector,
        later_directional_scales.reshape(1, -1),
        push_output_matrix.reshape(1, -1),
    )
    return tuple(jnp.transpose(result, (1, 0, 2)) for result in results)


def solution(mesh):
    along = P("groups", None, "dom")
    return jax.shard_map(
        on_device,
        mesh=mesh,
        in_specs=(
            along,
            along,
            P("groups"),
            P(("groups", "dom"), None),
            P("groups"),
            P("groups"),
            P(),
            P(),
            P(),
            P(),
            P(),
            P(),
            P(),
            P(),
        ),
        out_specs=(along, along, along),
        check_vma=False,
    )
```
